32 devices in a mesh: tm: 16 (over z, y, x), space: 2 (over core).
Axes of the slice: x: 2, y: 2, z: 4, core: 2. Of those that a mesh axis runs over, the one named last changes fastest.
Arguments:
- frames_feat: bfloat16 [16, 4, 64, 256], P('tm', 'space'), may hold values from -16 to 16
- prompt_labels: int32 [4, 64], P('space'), may hold values from 0 to 3
- label_table: float32 [4, 256], replicated, may hold values from -6 to 6
- enc_qkv: bfloat16 [256, 768], replicated, may hold values from -0.375 to 0.375
- enc_out: bfloat16 [256, 256], replicated, may hold values from -0.375 to 0.375
- norm_gain: float32 [256], replicated, may hold values from 0.25 to 1.75
- key_proj: bfloat16 [256, 1024], replicated, may hold values from -0.375 to 0.375
- value_proj: bfloat16 [256, 1024], replicated, may hold values from -0.375 to 0.375
- read_proj: bfloat16 [1024, 256], replicated, may hold values from -0.1875 to 0.1875
- decay: float32 [16, 8], P('tm'), may hold values from 0.1 to 1
- dec_conv: bfloat16 [3, 3, 256, 64], replicated, may hold values from -0.125 to 0.125
- dec_up: bfloat16 [64, 16], replicated, may hold values from -0.75 to 0.75
Outputs:
- mask_logits: float32 [16, 16, 256], P('tm', 'space')
The draws below stay inside these ranges and needn't reach their ends.
All inputs are finite; a program needn't handle non-finite values.
Results may differ from the reference program's by a relative error of at most 0.011.
The reference program's roundings to bfloat16 on the way count: a program that leaves them out, or rounds other values in their place, can miss the bound.
Values may be sent and summed in bfloat16 or wider, within the bound.
No kernel may reach another device: no remote copies, remote signals or barrier semaphores. Data moves between devices by JAX's collectives and lax.ppermute only.
A program may use at most 64 MiB of HBM per device.

```python
import math
import jax
import jax.numpy as jnp
from jax import lax

D = 256
ENC_HEADS = 8
MEMORY_HEADS = 8
KEY_FEATURES = 128
VAL_DIM = 128
DEC_CH = 64
LABELS = 4
UP = 4
GRID_W = 64
FRAME_COUNT = 16
GRID_H = 4


def draw_frames_feat(key, part):
    base_key = jax.random.fold_in(jax.random.fold_in(key, 301), 0)
    full_shape = (FRAME_COUNT, GRID_H, GRID_W, D)
    base_draw = jax.random.normal(base_key, full_shape, jnp.float32)
    values = base_draw
    return jnp.clip(values, -16.0, 16.0).astype(jnp.bfloat16)


def draw_decay(key, part):
    divided_keys = jax.random.split(jax.random.fold_in(key, 517), 6)
    head_pick = jax.random.randint(divided_keys[0], (MEMORY_HEADS,), 0, 8)
    slow_flag = head_pick >= 4
    slow_power = jax.random.uniform(divided_keys[1], (1, MEMORY_HEADS), jnp.float32, 0.05, 0.35)
    jitter = jax.random.uniform(divided_keys[2], (FRAME_COUNT, MEMORY_HEADS), jnp.float32, 0.5, 1.5)
    slow_rate = jnp.exp(math.log(0.1) * slow_power * jitter / FRAME_COUNT)
    fast_rate = jax.random.uniform(divided_keys[3], (FRAME_COUNT, MEMORY_HEADS), jnp.float32, 0.3, 0.75)
    decay_rates = jnp.where(slow_flag[None, :], slow_rate, fast_rate)
    surge_frames = jax.random.randint(divided_keys[4], (2,), 0, FRAME_COUNT)
    surge_mask = jnp.any(jnp.arange(FRAME_COUNT)[:, None] == surge_frames[None, :], axis=1)
    surge_multiplier = jax.random.uniform(divided_keys[5], (FRAME_COUNT, MEMORY_HEADS), jnp.float32, 0.55, 0.8)
    decay_rates = jnp.where(surge_mask[:, None], decay_rates * surge_multiplier, decay_rates)
    return jnp.clip(decay_rates, 0.1, 1.0).astype(jnp.float32)


def place_ends(result, own_key, low, largest):
    dims = result.shape
    spot = [jax.random.randint(jax.random.fold_in(own_key, axis), (), 0, dims[axis]) for axis in range(len(dims))]
    result = result.at[tuple(spot)].set(low)
    longest = dims.index(max(dims))
    spot[longest] = (spot[longest] + 1) % dims[longest]
    return result.at[tuple(spot)].set(largest)


def centred(key, extent, deviation, limit, held_as=jnp.bfloat16):
    array = jax.random.normal(key, extent, jnp.float32) * deviation
    return jnp.minimum(jnp.maximum(array, -limit), limit).astype(held_as)


def setup_inputs(seed: int = 0) -> dict:
    key_list = jax.random.split(jax.random.key(seed), 13)
    frames_feat = draw_frames_feat(jax.random.fold_in(key_list[12], 71), 0)
    prompt_labels = place_ends(jax.random.randint(key_list[1], (GRID_H, GRID_W), 0, LABELS), jax.random.fold_in(key_list[1], 1), 0, LABELS - 1).astype(jnp.int32)
    label_table = centred(key_list[2], (LABELS, D), 1.0, 6.0, jnp.float32)
    enc_qkv = centred(key_list[3], (D, 3 * D), D ** -0.5, 0.375)
    enc_out = centred(key_list[4], (D, D), D ** -0.5, 0.375)
    norm_gain = jnp.clip(1.0 + 0.15 * jax.random.normal(key_list[5], (D,), jnp.float32), 0.25, 1.75)
    key_proj = centred(key_list[6], (D, MEMORY_HEADS * KEY_FEATURES), D ** -0.5, 0.375)
    value_proj = centred(key_list[7], (D, MEMORY_HEADS * VAL_DIM), D ** -0.5, 0.375)
    read_proj = centred(key_list[8], (MEMORY_HEADS * VAL_DIM, D), (MEMORY_HEADS * VAL_DIM) ** -0.5, 0.1875)
    decay = draw_decay(jax.random.fold_in(key_list[12], 71), 0)
    dec_conv = centred(key_list[10], (3, 3, D, DEC_CH), (9 * D) ** -0.5, 0.125)
    dec_up = centred(key_list[11], (DEC_CH, UP * UP), DEC_CH ** -0.5, 0.75)
    return dict(frames_feat=frames_feat, prompt_labels=prompt_labels, label_table=label_table, enc_qkv=enc_qkv, enc_out=enc_out, norm_gain=norm_gain, key_proj=key_proj, value_proj=value_proj, read_proj=read_proj, decay=decay, dec_conv=dec_conv, dec_up=dec_up)


epsilon = 1e-06
precise_result = lax.Precision.HIGHEST

def pool_pairs(features):
    frame_count, height, breadth, channels = features.shape
    grouped = features.astype(jnp.float32).reshape(frame_count, height // 2, 2, breadth // 2, 2, channels)
    return lax.optimization_barrier(jnp.mean(grouped, axis=(2, 4))).astype(jnp.bfloat16)

def gain_norm(hidden, gain_row):
    return hidden * lax.rsqrt(lax.optimization_barrier(jnp.mean(hidden * hidden, axis=-1, keepdims=True)) + epsilon) * gain_row

def reference(frames_feat, prompt_labels, label_table, enc_qkv, enc_out, norm_gain, key_proj, value_proj, read_proj, decay, dec_conv, dec_up):
    head_size = D // ENC_HEADS
    frame_tokens = GRID_H * GRID_W
    flat_rows = frames_feat.reshape(FRAME_COUNT, frame_tokens, D)
    pooled = pool_pairs(frames_feat).reshape(FRAME_COUNT, frame_tokens // 4, D)

    def encode_frame(inputs):
        tok_rows, pooled_rows = inputs
        queries = jnp.dot(tok_rows, enc_qkv[:, :D], preferred_element_type=jnp.float32).astype(jnp.bfloat16)
        pair_kv = jnp.dot(pooled_rows, enc_qkv[:, D:], preferred_element_type=jnp.float32).astype(jnp.bfloat16)
        query_heads = queries.astype(jnp.float32).reshape(frame_tokens, ENC_HEADS, head_size)
        key_head_rows = pair_kv[:, :D].astype(jnp.float32).reshape(-1, ENC_HEADS, head_size)
        value_head_rows = pair_kv[:, D:].astype(jnp.float32).reshape(-1, ENC_HEADS, head_size)
        scores = jnp.einsum('tha,nha->htn', query_heads, key_head_rows, precision=precise_result) * head_size ** (-0.5)
        weights = jnp.exp(scores - lax.optimization_barrier(jnp.max(scores, axis=-1, keepdims=True)))
        totals = lax.optimization_barrier(jnp.sum(weights, axis=-1))
        rounded = lax.optimization_barrier(weights.astype(jnp.bfloat16)).astype(jnp.float32)
        attended = jnp.einsum('htn,nha->hta', rounded, value_head_rows, precision=precise_result) / totals[..., None]
        attended = attended.transpose(1, 0, 2).reshape(frame_tokens, D).astype(jnp.bfloat16)
        hidden = tok_rows.astype(jnp.float32) + jnp.dot(attended, enc_out, preferred_element_type=jnp.float32)
        return gain_norm(hidden, norm_gain).astype(jnp.bfloat16)
    encoded = lax.map(encode_frame, (flat_rows, pooled))
    label_rows = label_table[prompt_labels.reshape(frame_tokens)]
    first_flag = (jnp.arange(FRAME_COUNT) == 0).astype(jnp.float32)

    def frame_state(inputs):
        encoded_rows, flag_value = inputs
        key_rows = jnp.dot(encoded_rows, key_proj, preferred_element_type=jnp.float32).astype(jnp.bfloat16)
        memory_in = (encoded_rows.astype(jnp.float32) + flag_value * label_rows).astype(jnp.bfloat16)
        value_rows = jnp.dot(memory_in, value_proj, preferred_element_type=jnp.float32).astype(jnp.bfloat16)
        key_head_rows = key_rows.astype(jnp.float32).reshape(frame_tokens, MEMORY_HEADS, KEY_FEATURES)
        value_head_rows = value_rows.astype(jnp.float32).reshape(frame_tokens, MEMORY_HEADS, VAL_DIM)
        cleared_state = jnp.einsum('gmp,gmz->mpz', key_head_rows, value_head_rows, precision=precise_result) * frame_tokens ** (-0.5)
        return (key_rows, cleared_state)
    key_rows, states = lax.map(frame_state, (encoded, first_flag))

    def advance(carried, inputs):
        rate_row, cleared_state = inputs
        memory = rate_row[:, None, None] * carried
        return (memory + cleared_state, memory)
    zero_state = jnp.zeros((MEMORY_HEADS, KEY_FEATURES, VAL_DIM), jnp.float32)
    _, memory = lax.scan(advance, zero_state, (decay, states))

    def read_frame(inputs):
        frame_keys, encoded_rows, memory_now = inputs
        truncated_memory = lax.optimization_barrier(memory_now.astype(jnp.bfloat16)).astype(jnp.float32)
        key_head_rows = frame_keys.astype(jnp.float32).reshape(frame_tokens, MEMORY_HEADS, KEY_FEATURES)
        memory_output = jnp.einsum('gba,ban->gbn', key_head_rows, truncated_memory, precision=precise_result) * KEY_FEATURES ** (-0.5)
        memory_output = memory_output.reshape(frame_tokens, MEMORY_HEADS * VAL_DIM).astype(jnp.bfloat16)
        joined_rows = encoded_rows.astype(jnp.float32) + jnp.dot(memory_output, read_proj, preferred_element_type=jnp.float32)
        return joined_rows.astype(jnp.bfloat16)
    decoder_in = lax.map(read_frame, (key_rows, encoded, memory)).reshape(FRAME_COUNT, GRID_H, GRID_W, D)

    def decode_frame(plane_rows):
        padded = jnp.pad(plane_rows, ((1, 1), (1, 1), (0, 0)))
        convolved = jnp.zeros((GRID_H * GRID_W, DEC_CH), jnp.float32)
        for row_shift in range(3):
            for col_shift in range(3):
                window = padded[row_shift:row_shift + GRID_H, col_shift:col_shift + GRID_W, :].reshape(GRID_H * GRID_W, D)
                convolved = convolved + jnp.dot(window, dec_conv[row_shift, col_shift], preferred_element_type=jnp.float32)
        mapped = jax.nn.gelu(convolved).astype(jnp.bfloat16)
        pixels = jnp.dot(mapped, dec_up, preferred_element_type=jnp.float32).reshape(GRID_H, GRID_W, UP, UP)
        return pixels.transpose(0, 2, 1, 3).reshape(GRID_H * UP, GRID_W * UP)
    return lax.map(decode_frame, decoder_in)
```

```python
import functools

import jax
import jax.numpy as jnp
import numpy as np
from jax import lax
from jax.experimental import pallas as pl
from jax.experimental.pallas import tpu as pltpu
from jax.sharding import PartitionSpec as P

ENC_HEADS = 8
UP = 4
LANES = 128
EPSILON = 1e-06
F32 = jnp.float32
BF16 = jnp.bfloat16
VMEM = pl.BlockSpec(memory_space=pltpu.VMEM)


def dot(a, b):
    return jnp.dot(a, b, preferred_element_type=F32)


def dot_on(a, b, dim_a, dim_b, precision=None):
    return lax.dot_general(
        a, b, (((dim_a,), (dim_b,)), ((), ())), precision=precision, preferred_element_type=F32
    )


def call(body, outs, scratch=()):
    return pl.pallas_call(
        body,
        out_shape=outs,
        out_specs=jax.tree.map(lambda _: VMEM, outs),
        scratch_shapes=scratch,
    )


def carry_rows(share):
    return -(-3 * share // 16) * 16


def write_payload(pay_ref, totals, product, share, key_dim):
    for h in range(share):
        rows = slice(h * key_dim, (h + 1) * key_dim)
        pay_ref[rows, :] = totals[h].astype(BF16)
    high = product.astype(BF16)
    rest = product - high.astype(F32)
    mid = rest.astype(BF16)
    low = (rest - mid.astype(F32)).astype(BF16)
    tail = carry_rows(share)
    parts = [high.astype(F32), mid.astype(F32), low.astype(F32)]
    if tail > 3 * share:
        parts.append(jnp.zeros((tail - 3 * share, product.shape[1]), F32))
    pay_ref[share * key_dim :, :] = jnp.concatenate(parts, axis=0).astype(BF16)


def encode_body(
    width,
    tile_tok,
    share,
    x_ref,
    label_ref,
    table_ref,
    pool_ref,
    qkv_ref,
    out_ref,
    gain_ref,
    key_ref,
    value_ref,
    decay_ref,
    window_ref,
    state_ref,
    pay_ref,
    padded,
):
    tokens, dim = x_ref.shape
    size = dim // ENC_HEADS
    place = lax.axis_index("space")
    x = x_ref[...]
    pooled = dot(pool_ref[...], x).astype(BF16)
    pair = dot(pooled, qkv_ref[:, dim:]).astype(BF16)
    queries = dot(x, qkv_ref[:, :dim]).astype(BF16)
    count = pooled.shape[0]
    lane = lax.broadcasted_iota(jnp.int32, (count, dim), 1)
    masks = [(lane >= h * size) & (lane < (h + 1) * size) for h in range(ENC_HEADS)]
    zero = jnp.zeros((count, dim), BF16)
    keys = jnp.concatenate([jnp.where(m, pair[:, :dim], zero) for m in masks], axis=0)
    values = jnp.concatenate([jnp.where(m, pair[:, dim:], zero) for m in masks], axis=0)
    scores = (dot_on(keys, queries, 1, 1) * size ** (-0.5)).reshape(ENC_HEADS, count, tokens)
    weights = jnp.exp(scores - jnp.max(scores, axis=1, keepdims=True))
    totals = jnp.sum(weights, axis=1, keepdims=True)
    rounded = weights.astype(BF16).reshape(ENC_HEADS * count, tokens)
    summed = dot_on(values, rounded, 0, 0).reshape(ENC_HEADS, size, tokens)
    attended = (summed / totals).reshape(dim, tokens).astype(BF16)
    hidden = x.astype(F32) + dot_on(attended, out_ref[...], 0, 0)
    scale = lax.rsqrt(jnp.mean(hidden * hidden, axis=-1, keepdims=True) + EPSILON)
    encoded = (hidden * scale * gain_ref[...]).astype(BF16)
    edge = jnp.zeros((width, dim), BF16)
    padded[:width, :] = edge
    padded[width : width + tokens, :] = encoded
    padded[width + tokens :, :] = edge
    start = pl.multiple_of(place * tile_tok, width)
    window_ref[...] = padded[pl.ds(start, tile_tok + 2 * width), :]

    flag = (lax.axis_index("tm") == 0).astype(F32)
    kinds = table_ref.shape[0]
    kind = lax.broadcasted_iota(jnp.int32, (kinds, tokens), 0)
    one_hot = (jnp.broadcast_to(label_ref[...], (kinds, tokens)) == kind).astype(F32)
    label_rows = dot_on(one_hot, table_ref[...], 0, 0, lax.Precision.HIGHEST)
    memory_in = (encoded.astype(F32) + flag * label_rows).astype(BF16)
    cols = key_ref.shape[1] // lax.axis_size("space")
    val_cols = value_ref.shape[1] // lax.axis_size("space")
    key_start = pl.multiple_of(place * cols, LANES)
    val_start = pl.multiple_of(place * val_cols, LANES)
    own_keys = dot(encoded, key_ref[:, pl.ds(key_start, cols)]).astype(BF16)
    own_values = dot(memory_in, value_ref[:, pl.ds(val_start, val_cols)]).astype(BF16)
    key_dim, val_dim = cols // share, val_cols // share
    states = []
    for h in range(share):
        state = dot_on(
            own_keys[:, h * key_dim : (h + 1) * key_dim],
            own_values[:, h * val_dim : (h + 1) * val_dim],
            0,
            0,
        ) * tokens ** (-0.5)
        state_ref[h * key_dim : (h + 1) * key_dim, :] = state
        states.append(state)
    write_payload(pay_ref, states, decay_ref[...], share, key_dim)


def combine_body(bit, share, first, last, recv_ref, total_ref, product_ref, *refs):
    if first:
        rate_ref = product_ref
        outs = refs
    else:
        reach_ref, prefix_ref = refs[:2]
        outs = refs[2:]
    rows = total_ref.shape[0]
    key_dim = rows // share
    upper = (lax.axis_index("tm") >> bit) & 1
    is_upper = jnp.full(product_ref.shape, upper, jnp.int32) == 1
    product = product_ref[...]
    reach = product if first else reach_ref[...]
    tail = recv_ref[rows:, :].astype(F32)
    got = tail[:share] + tail[share : 2 * share] + tail[2 * share : 3 * share]
    ones = jnp.ones_like(product)
    on_got = jnp.where(is_upper, product, ones)
    on_own = jnp.where(is_upper, ones, got)
    on_prefix = jnp.where(is_upper, reach, jnp.zeros_like(product))
    totals = []
    for h in range(share):
        part = slice(h * key_dim, (h + 1) * key_dim)
        arrived = recv_ref[part, :].astype(F32)
        prefix = on_prefix[h : h + 1] * arrived
        if not first:
            prefix = prefix + prefix_ref[part, :]
        if last:
            outs[0][part, :] = prefix.astype(BF16)
        else:
            outs[3][part, :] = prefix
            total = on_got[h : h + 1] * arrived + on_own[h : h + 1] * total_ref[part, :]
            totals.append(total)
            outs[0][part, :] = total
    if not last:
        joined = product * got
        outs[1][...] = joined
        outs[2][...] = jnp.where(is_upper, reach * got, reach)
        write_payload(outs[4], totals, joined, share, key_dim)


def keys_body(window_ref, key_ref, out_ref):
    out_ref[...] = dot(window_ref[...], key_ref[...]).astype(BF16)


def decode_body(
    width, heads, key_ref, window_ref, memory_ref, read_ref, conv_ref, up_ref, spread_ref, out_ref
):
    rows, dim = window_ref.shape
    tile_tok = rows - 2 * width
    key_dim = key_ref.shape[1] // heads
    reads = [
        (
            dot(
                key_ref[:, h * key_dim : (h + 1) * key_dim],
                memory_ref[h * key_dim : (h + 1) * key_dim, :],
            )
            * key_dim ** (-0.5)
        ).astype(BF16)
        for h in range(heads)
    ]
    readout = jnp.concatenate(reads, axis=1)
    joined = (window_ref[...].astype(F32) + dot(readout, read_ref[...])).astype(BF16)
    columns = []
    for b in range(3):
        total = dot(joined[:tile_tok], conv_ref[0, b])
        for a in range(1, 3):
            total = total + dot(joined[a * width : a * width + tile_tok], conv_ref[a, b])
        columns.append(total)
    col = lax.broadcasted_iota(jnp.int32, columns[0].shape, 0) % width
    zero = jnp.zeros_like(columns[0])
    left = jnp.where(col == 0, zero, pltpu.roll(columns[0], 1, 0))
    right = jnp.where(col == width - 1, zero, pltpu.roll(columns[2], tile_tok - 1, 0))
    mapped = jax.nn.gelu(left + columns[1] + right).astype(BF16)
    wide = width * UP
    lane = lax.broadcasted_iota(jnp.int32, (UP, UP, wide), 2)
    sub = lax.broadcasted_iota(jnp.int32, (UP, UP, wide), 1)
    chosen = (lane % UP) == sub
    for i in range(tile_tok // width):
        hidden = dot(spread_ref[...], mapped[i * width : (i + 1) * width]).astype(BF16)
        pixels = dot_on(up_ref[...], hidden, 0, 1).reshape(UP, UP, wide)
        picked = jnp.sum(jnp.where(chosen, pixels, jnp.zeros_like(pixels)), axis=1)
        out_ref[i * UP : (i + 1) * UP, :] = picked


def shards(
    frames_feat,
    prompt_labels,
    label_table,
    enc_qkv,
    enc_out,
    norm_gain,
    key_proj,
    value_proj,
    read_proj,
    decay,
    dec_conv,
    dec_up,
):
    _, tile_rows, width, dim = frames_feat.shape
    tile_tok = tile_rows * width
    bands, frames = lax.axis_size("space"), lax.axis_size("tm")
    tokens = tile_tok * bands
    heads = decay.shape[1]
    share = heads // bands
    key_dim, val_dim = key_proj.shape[1] // heads, value_proj.shape[1] // heads
    rows = share * key_dim
    window_rows = tile_tok + 2 * width
    sds = jax.ShapeDtypeStruct

    flat = frames_feat.reshape(tile_tok, dim)
    frame = lax.all_gather(flat, "space", axis=0, tiled=True)
    labels = lax.all_gather(prompt_labels.reshape(1, tile_tok), "space", axis=1, tiled=True)
    rate = lax.dynamic_slice_in_dim(decay, lax.axis_index("space") * share, share, 1)
    rate = jnp.broadcast_to(rate.reshape(share, 1), (share, val_dim))

    token = np.arange(tokens)
    cell = (token // width // 2) * (width // 2) + token % width // 2
    pool = jnp.asarray((cell[None, :] == np.arange(tokens // 4)[:, None]) * 0.25, BF16)
    wide = np.arange(width * UP)
    spread = jnp.asarray((wide[:, None] // UP) == np.arange(width)[None, :], BF16)

    pay = sds((rows + carry_rows(share), val_dim), BF16)
    state = sds((rows, val_dim), F32)
    small = sds((share, val_dim), F32)
    window, total, payload = call(
        functools.partial(encode_body, width, tile_tok, share),
        (sds((window_rows, dim), BF16), state, pay),
        (pltpu.VMEM((tokens + 2 * width, dim), BF16),),
    )(
        frame,
        labels,
        label_table,
        pool,
        enc_qkv,
        enc_out,
        norm_gain.reshape(1, dim),
        key_proj,
        value_proj,
        rate,
    )
    product, carried = rate, ()
    steps = (frames - 1).bit_length()
    key_rows = None
    for bit in range(steps):
        first, last = bit == 0, bit == steps - 1
        pairs = [(i, i ^ (1 << bit)) for i in range(frames) if i ^ (1 << bit) < frames]
        arrived = lax.ppermute(payload, "tm", pairs)
        if first:
            key_rows = call(keys_body, sds((window_rows, heads * key_dim), BF16))(window, key_proj)
        body = functools.partial(combine_body, bit, share, first, last)
        if last:
            memory = call(body, sds((rows, val_dim), BF16))(arrived, total, product, *carried)
        else:
            total, product, reach, prefix, payload = call(body, (state, small, small, state, pay))(
                arrived, total, product, *carried
            )
            carried = (reach, prefix)
    memory = lax.all_gather(memory, "space", axis=0, tiled=True)
    logits = call(
        functools.partial(decode_body, width, heads),
        sds((tile_rows * UP, width * UP), F32),
    )(key_rows, window, memory, read_proj, dec_conv, dec_up, spread)
    return logits[None]


def solution(mesh):
    return jax.shard_map(
        shards,
        mesh=mesh,
        in_specs=(
            P("tm", "space", None, None),
            P("space", None),
            P(),
            P(),
            P(),
            P(),
            P(),
            P(),
            P(),
            P("tm", None),
            P(),
            P(),
        ),
        out_specs=P("tm", "space", None),
        check_vma=False,
    )
```

```python
import functools

import jax
import jax.numpy as jnp
import numpy as np
from jax import lax
from jax.experimental import pallas as pl
from jax.experimental.pallas import tpu as pltpu
from jax.sharding import PartitionSpec as P

ENC_HEADS = 8
UP = 4
LANES = 128
EPSILON = 1e-06
F32 = jnp.float32
BF16 = jnp.bfloat16
VMEM = pl.BlockSpec(memory_space=pltpu.VMEM)


def dot(a, b):
    return jnp.dot(a, b, preferred_element_type=F32)


def dot_on(a, b, dim_a, dim_b, precision=None):
    return lax.dot_general(
        a, b, (((dim_a,), (dim_b,)), ((), ())), precision=precision, preferred_element_type=F32
    )


def call(body, outs, scratch=(), spaces=None):
    def on_chip(*operands):
        places = [pltpu.VMEM] * len(operands) if spaces is None else spaces
        run = pl.pallas_call(
            body,
            out_shape=outs,
            in_specs=[pl.BlockSpec(memory_space=place) for place in places],
            out_specs=jax.tree.map(lambda _: VMEM, outs),
            scratch_shapes=scratch,
        )
        return run(
            *[
                pltpu.with_memory_space_constraint(x, place) if place is pltpu.VMEM else x
                for x, place in zip(operands, places)
            ]
        )

    return on_chip


def carry_rows(share):
    return -(-3 * share // 16) * 16


def write_payload(pay_ref, totals, product, share, key_dim):
    for h in range(share):
        rows = slice(h * key_dim, (h + 1) * key_dim)
        pay_ref[rows, :] = totals[h].astype(BF16)
    high = product.astype(BF16)
    rest = product - high.astype(F32)
    mid = rest.astype(BF16)
    low = (rest - mid.astype(F32)).astype(BF16)
    tail = carry_rows(share)
    parts = [high.astype(F32), mid.astype(F32), low.astype(F32)]
    if tail > 3 * share:
        parts.append(jnp.zeros((tail - 3 * share, product.shape[1]), F32))
    pay_ref[share * key_dim :, :] = jnp.concatenate(parts, axis=0).astype(BF16)


def encode_body(width, share, parts, *refs):
    tiles, labels = refs[:parts], refs[parts : 2 * parts]
    table_ref, gain_ref, decay_ref = refs[2 * parts : 2 * parts + 3]
    pool_hbm, qkv_hbm, out_hbm, key_hbm, value_hbm = refs[2 * parts + 3 : 2 * parts + 8]
    window_ref, state_ref, product_ref, pay_ref = refs[2 * parts + 8 : 2 * parts + 12]
    padded, tile_ref, pool_ref, qkv_ref, out_ref, key_ref, value_ref, sems = refs[2 * parts + 12 :]
    place = lax.axis_index("space")
    cols, val_cols = key_ref.shape[1], value_ref.shape[1]
    key_start = pl.multiple_of(place * cols, LANES)
    val_start = pl.multiple_of(place * val_cols, LANES)
    loads = [
        pltpu.make_async_copy(source, target, sems.at[n])
        for n, (source, target) in enumerate(
            (
                (tiles[0], tile_ref),
                (pool_hbm, pool_ref),
                (qkv_hbm, qkv_ref),
                (out_hbm, out_ref),
                (key_hbm.at[:, pl.ds(key_start, cols)], key_ref),
                (value_hbm.at[:, pl.ds(val_start, val_cols)], value_ref),
            )
        )
    ]
    for load in loads:
        load.start()
    loads[0].wait()
    x = jnp.concatenate([tile_ref[...]] + [tile[...] for tile in tiles[1:]], axis=0)
    tokens, dim = x.shape
    size = dim // ENC_HEADS
    window_rows = window_ref.shape[0]
    tile_tok = window_rows - 2 * width
    loads[1].wait()
    pooled = dot(pool_ref[...], x).astype(BF16)
    loads[2].wait()
    pair = dot(pooled, qkv_ref[:, dim:]).astype(BF16)
    queries = dot(x, qkv_ref[:, :dim]).astype(BF16)
    count = pooled.shape[0]
    lane = lax.broadcasted_iota(jnp.int32, (count, dim), 1)
    masks = [(lane >= h * size) & (lane < (h + 1) * size) for h in range(ENC_HEADS)]
    zero = jnp.zeros((count, dim), BF16)
    keys = jnp.concatenate([jnp.where(m, pair[:, :dim], zero) for m in masks], axis=0)
    values = jnp.concatenate([jnp.where(m, pair[:, dim:], zero) for m in masks], axis=0)
    scores = (dot_on(keys, queries, 1, 1) * size ** (-0.5)).reshape(ENC_HEADS, count, tokens)
    weights = jnp.exp(scores - jnp.max(scores, axis=1, keepdims=True))
    totals = jnp.sum(weights, axis=1, keepdims=True)
    rounded = weights.astype(BF16).reshape(ENC_HEADS * count, tokens)
    summed = dot_on(values, rounded, 0, 0).reshape(ENC_HEADS, size, tokens)
    attended = (summed / totals).reshape(dim, tokens).astype(BF16)
    loads[3].wait()
    hidden = x.astype(F32) + dot_on(attended, out_ref[...], 0, 0)
    scale = lax.rsqrt(jnp.mean(hidden * hidden, axis=-1, keepdims=True) + EPSILON)
    encoded = (hidden * scale * gain_ref[...]).astype(BF16)
    edge = jnp.zeros((width, dim), BF16)
    padded[:width, :] = edge
    padded[width + tokens :, :] = edge
    for p in range(parts):
        spot = place if p == 0 else 1 - place
        spot = pl.multiple_of(width + spot * tile_tok, width) if parts > 1 else width
        rows = tokens // parts
        padded[pl.ds(spot, rows), :] = encoded[p * rows : (p + 1) * rows]
    window_ref[...] = padded[pl.ds(pl.multiple_of(place * tile_tok, width), window_rows), :]

    flag = (lax.axis_index("tm") == 0).astype(F32)
    kinds = table_ref.shape[0]
    label = jnp.concatenate([ref[...] for ref in labels], axis=1)
    kind = lax.broadcasted_iota(jnp.int32, (kinds, tokens), 0)
    one_hot = (jnp.broadcast_to(label, (kinds, tokens)) == kind).astype(F32)
    label_rows = dot_on(one_hot, table_ref[...], 0, 0, lax.Precision.HIGHEST)
    memory_in = (encoded.astype(F32) + flag * label_rows).astype(BF16)
    loads[4].wait()
    own_keys = dot(encoded, key_ref[...]).astype(BF16)
    loads[5].wait()
    own_values = dot(memory_in, value_ref[...]).astype(BF16)
    key_dim, val_dim = cols // share, val_cols // share
    states = []
    for h in range(share):
        state = dot_on(
            own_keys[:, h * key_dim : (h + 1) * key_dim],
            own_values[:, h * val_dim : (h + 1) * val_dim],
            0,
            0,
        ) * tokens ** (-0.5)
        state_ref[h * key_dim : (h + 1) * key_dim, :] = state
        states.append(state)
    product = jnp.concatenate(
        [jnp.full((1, val_dim), decay_ref[0, place * share + h], F32) for h in range(share)], axis=0
    )
    product_ref[...] = product
    write_payload(pay_ref, states, product, share, key_dim)


def combine_body(bit, share, first, last, recv_ref, total_ref, product_ref, *refs):
    if first:
        rate_ref = product_ref
        outs = refs
    else:
        reach_ref, prefix_ref = refs[:2]
        outs = refs[2:]
    rows = total_ref.shape[0]
    key_dim = rows // share
    upper = (lax.axis_index("tm") >> bit) & 1
    is_upper = jnp.full(product_ref.shape, upper, jnp.int32) == 1
    product = product_ref[...]
    reach = product if first else reach_ref[...]
    tail = recv_ref[rows:, :].astype(F32)
    got = tail[:share] + tail[share : 2 * share] + tail[2 * share : 3 * share]
    ones = jnp.ones_like(product)
    on_got = jnp.where(is_upper, product, ones)
    on_own = jnp.where(is_upper, ones, got)
    on_prefix = jnp.where(is_upper, reach, jnp.zeros_like(product))
    totals = []
    for h in range(share):
        part = slice(h * key_dim, (h + 1) * key_dim)
        arrived = recv_ref[part, :].astype(F32)
        prefix = on_prefix[h : h + 1] * arrived
        if not first:
            prefix = prefix + prefix_ref[part, :]
        if last:
            outs[0][part, :] = prefix.astype(BF16)
        else:
            outs[3][part, :] = prefix
            total = on_got[h : h + 1] * arrived + on_own[h : h + 1] * total_ref[part, :]
            totals.append(total)
            outs[0][part, :] = total
    if not last:
        joined = product * got
        outs[1][...] = joined
        outs[2][...] = jnp.where(is_upper, reach * got, reach)
        write_payload(outs[4], totals, joined, share, key_dim)


def keys_body(window_ref, key_ref, out_ref):
    out_ref[...] = dot(window_ref[...], key_ref[...]).astype(BF16)


def decode_body(
    width, heads, key_ref, window_ref, memory_ref, read_ref, conv_ref, up_ref, spread_ref, out_ref
):
    rows, dim = window_ref.shape
    tile_tok = rows - 2 * width
    key_dim = key_ref.shape[1] // heads
    reads = [
        (
            dot(
                key_ref[:, h * key_dim : (h + 1) * key_dim],
                memory_ref[h * key_dim : (h + 1) * key_dim, :],
            )
            * key_dim ** (-0.5)
        ).astype(BF16)
        for h in range(heads)
    ]
    readout = jnp.concatenate(reads, axis=1)
    joined = (window_ref[...].astype(F32) + dot(readout, read_ref[...])).astype(BF16)
    columns = []
    for b in range(3):
        total = dot_on(joined[:tile_tok], conv_ref[0, b], 1, 1)
        for a in range(1, 3):
            total = total + dot_on(
                joined[a * width : a * width + tile_tok], conv_ref[a, b], 1, 1
            )
        columns.append(total)
    col = lax.broadcasted_iota(jnp.int32, columns[0].shape, 0) % width
    zero = jnp.zeros_like(columns[0])
    left = jnp.where(col == 0, zero, pltpu.roll(columns[0], 1, 0))
    right = jnp.where(col == width - 1, zero, pltpu.roll(columns[2], tile_tok - 1, 0))
    mapped = jax.nn.gelu(left + columns[1] + right).astype(BF16)
    wide = width * UP
    lane = lax.broadcasted_iota(jnp.int32, (UP, UP, wide), 2)
    sub = lax.broadcasted_iota(jnp.int32, (UP, UP, wide), 1)
    chosen = (lane % UP) == sub
    for i in range(tile_tok // width):
        hidden = dot(spread_ref[...], mapped[i * width : (i + 1) * width]).astype(BF16)
        pixels = dot_on(up_ref[...], hidden, 1, 1).reshape(UP, UP, wide)
        picked = jnp.sum(jnp.where(chosen, pixels, jnp.zeros_like(pixels)), axis=1)
        out_ref[i * UP : (i + 1) * UP, :] = picked


def shards(
    frames_feat,
    prompt_labels,
    label_table,
    enc_qkv,
    enc_out,
    norm_gain,
    key_proj,
    value_proj,
    read_proj,
    decay,
    dec_conv,
    dec_up,
):
    _, tile_rows, width, dim = frames_feat.shape
    tile_tok = tile_rows * width
    bands, frames = lax.axis_size("space"), lax.axis_size("tm")
    tokens = tile_tok * bands
    heads = decay.shape[1]
    share = heads // bands
    key_dim, val_dim = key_proj.shape[1] // heads, value_proj.shape[1] // heads
    rows = share * key_dim
    window_rows = tile_tok + 2 * width
    sds = pltpu.VMEM

    flat = frames_feat.reshape(tile_tok, dim)
    labels = prompt_labels.reshape(1, tile_tok)
    if bands == 2:
        swap = [(0, 1), (1, 0)]
        tiles = [flat, lax.ppermute(flat, "space", swap)]
        marks = [labels, lax.ppermute(labels, "space", swap)]
    else:
        tiles = [lax.all_gather(flat, "space", axis=0, tiled=True)]
        marks = [lax.all_gather(labels, "space", axis=1, tiled=True)]

    token = np.arange(tokens)
    cell = (token // width // 2) * (width // 2) + token % width // 2
    pool = jnp.asarray((cell[None, :] == np.arange(tokens // 4)[:, None]) * 0.25, BF16)
    wide = np.arange(width * UP)
    spread = jnp.asarray((wide[:, None] // UP) == np.arange(width)[None, :], BF16)

    pay = sds((rows + carry_rows(share), val_dim), BF16)
    state = sds((rows, val_dim), F32)
    small = sds((share, val_dim), F32)
    parts = len(tiles)
    key_cols, val_cols = share * key_dim, share * val_dim
    window, total, product, payload = call(
        functools.partial(encode_body, width, share, parts),
        (sds((window_rows, dim), BF16), state, small, pay),
        (
            pltpu.VMEM((tokens + 2 * width, dim), BF16),
            pltpu.VMEM(tiles[0].shape, BF16),
            pltpu.VMEM(pool.shape, BF16),
            pltpu.VMEM(enc_qkv.shape, BF16),
            pltpu.VMEM(enc_out.shape, BF16),
            pltpu.VMEM((dim, key_cols), BF16),
            pltpu.VMEM((dim, val_cols), BF16),
            pltpu.SemaphoreType.DMA((6,)),
        ),
        [pl.ANY] + [pltpu.VMEM] * (2 * parts + 1) + [pltpu.SMEM] + [pl.ANY] * 5,
    )(
        *tiles,
        *marks,
        label_table,
        norm_gain.reshape(1, dim),
        decay,
        pool,
        enc_qkv,
        enc_out,
        key_proj,
        value_proj,
    )
    carried = ()
    steps = (frames - 1).bit_length()
    key_rows = None
    for bit in range(steps):
        first, last = bit == 0, bit == steps - 1
        pairs = [(i, i ^ (1 << bit)) for i in range(frames) if i ^ (1 << bit) < frames]
        arrived = lax.ppermute(payload, "tm", pairs)
        if first:
            key_rows = call(keys_body, sds((window_rows, heads * key_dim), BF16))(window, key_proj)
        body = functools.partial(combine_body, bit, share, first, last)
        if last:
            memory = call(body, sds((rows, val_dim), BF16))(arrived, total, product, *carried)
        else:
            total, product, reach, prefix, payload = call(body, (state, small, small, state, pay))(
                arrived, total, product, *carried
            )
            carried = (reach, prefix)
    memory = lax.all_gather(memory, "space", axis=0, tiled=True)
    logits = call(
        functools.partial(decode_body, width, heads),
        jax.ShapeDtypeStruct((tile_rows * UP, width * UP), F32),
    )(key_rows, window, memory, read_proj, dec_conv.swapaxes(2, 3), dec_up.T, spread)
    return logits[None]


def solution(mesh):
    return jax.shard_map(
        shards,
        mesh=mesh,
        in_specs=(
            P("tm", "space", None, None),
            P("space", None),
            P(),
            P(),
            P(),
            P(),
            P(),
            P(),
            P(),
            P("tm", None),
            P(),
            P(),
        ),
        out_specs=P("tm", "space", None),
        check_vma=False,
    )
```

```python
import functools

import jax
import jax.numpy as jnp
import numpy as np
from jax import lax
from jax.experimental import pallas as pl
from jax.experimental.pallas import tpu as pltpu
from jax.sharding import PartitionSpec as P

ENC_HEADS = 8
UP = 4
LANES = 128
EPSILON = 1e-06
F32 = jnp.float32
BF16 = jnp.bfloat16
VMEM = pl.BlockSpec(memory_space=pltpu.VMEM)


def dot(a, b):
    return jnp.dot(a, b, preferred_element_type=F32)


def dot_on(a, b, dim_a, dim_b, precision=None):
    return lax.dot_general(
        a, b, (((dim_a,), (dim_b,)), ((), ())), precision=precision, preferred_element_type=F32
    )


def call(body, outs, scratch=(), spaces=None):
    def on_chip(*operands):
        places = [pltpu.VMEM] * len(operands) if spaces is None else spaces
        run = pl.pallas_call(
            body,
            out_shape=outs,
            in_specs=[pl.BlockSpec(memory_space=place) for place in places],
            out_specs=jax.tree.map(lambda _: VMEM, outs),
            scratch_shapes=scratch,
        )
        return run(
            *[
                pltpu.with_memory_space_constraint(x, place) if place is pltpu.VMEM else x
                for x, place in zip(operands, places)
            ]
        )

    return on_chip


def carry_rows(share):
    return -(-3 * share // 16) * 16


def write_payload(pay_ref, totals, product, share, key_dim):
    for h in range(share):
        rows = slice(h * key_dim, (h + 1) * key_dim)
        pay_ref[rows, :] = totals[h].astype(BF16)
    high = product.astype(BF16)
    rest = product - high.astype(F32)
    mid = rest.astype(BF16)
    low = (rest - mid.astype(F32)).astype(BF16)
    tail = carry_rows(share)
    parts = [high.astype(F32), mid.astype(F32), low.astype(F32)]
    if tail > 3 * share:
        parts.append(jnp.zeros((tail - 3 * share, product.shape[1]), F32))
    pay_ref[share * key_dim :, :] = jnp.concatenate(parts, axis=0).astype(BF16)


def encode_body(width, parts, *refs):
    tiles, labels = refs[:parts], refs[parts : 2 * parts]
    rest = refs[2 * parts :]
    table_ref, gain_ref, pool_hbm, qkv_hbm, out_hbm, key_hbm, value_hbm = rest[:7]
    window_ref, encoded_ref, memory_ref, key_ref, value_ref = rest[7:12]
    padded, tile_ref, pool_ref, qkv_ref, out_ref, sems = rest[12:]
    place = lax.axis_index("space")
    cols, val_cols = key_ref.shape[1], value_ref.shape[1]
    key_start = pl.multiple_of(place * cols, LANES)
    val_start = pl.multiple_of(place * val_cols, LANES)
    loads = [
        pltpu.make_async_copy(source, target, sems.at[n])
        for n, (source, target) in enumerate(
            (
                (tiles[0], tile_ref),
                (pool_hbm, pool_ref),
                (qkv_hbm, qkv_ref),
                (out_hbm, out_ref),
                (key_hbm.at[:, pl.ds(key_start, cols)], key_ref),
                (value_hbm.at[:, pl.ds(val_start, val_cols)], value_ref),
            )
        )
    ]
    for load in loads:
        load.start()
    loads[0].wait()
    x = jnp.concatenate([tile_ref[...]] + [tile[...] for tile in tiles[1:]], axis=0)
    tokens, dim = x.shape
    size = dim // ENC_HEADS
    window_rows = window_ref.shape[0]
    tile_tok = window_rows - 2 * width
    loads[1].wait()
    pooled = dot(pool_ref[...], x).astype(BF16)
    loads[2].wait()
    pair = dot(pooled, qkv_ref[:, dim:]).astype(BF16)
    queries = dot(x, qkv_ref[:, :dim]).astype(BF16)
    count = pooled.shape[0]
    lane = lax.broadcasted_iota(jnp.int32, (count, dim), 1)
    masks = [(lane >= h * size) & (lane < (h + 1) * size) for h in range(ENC_HEADS)]
    zero = jnp.zeros((count, dim), BF16)
    keys = jnp.concatenate([jnp.where(m, pair[:, :dim], zero) for m in masks], axis=0)
    values = jnp.concatenate([jnp.where(m, pair[:, dim:], zero) for m in masks], axis=0)
    scores = (dot_on(keys, queries, 1, 1) * size ** (-0.5)).reshape(ENC_HEADS, count, tokens)
    weights = jnp.exp(scores - jnp.max(scores, axis=1, keepdims=True))
    totals = jnp.sum(weights, axis=1, keepdims=True)
    rounded = weights.astype(BF16).reshape(ENC_HEADS * count, tokens)
    summed = dot_on(values, rounded, 0, 0).reshape(ENC_HEADS, size, tokens)
    attended = (summed / totals).reshape(dim, tokens).astype(BF16)
    loads[3].wait()
    hidden = x.astype(F32) + dot_on(attended, out_ref[...], 0, 0)
    scale = lax.rsqrt(jnp.mean(hidden * hidden, axis=-1, keepdims=True) + EPSILON)
    encoded = (hidden * scale * gain_ref[...]).astype(BF16)
    edge = jnp.zeros((width, dim), BF16)
    padded[:width, :] = edge
    padded[width + tokens :, :] = edge
    for p in range(parts):
        spot = place if p == 0 else 1 - place
        spot = pl.multiple_of(width + spot * tile_tok, width) if parts > 1 else width
        rows = tokens // parts
        padded[pl.ds(spot, rows), :] = encoded[p * rows : (p + 1) * rows]
    window_ref[...] = padded[pl.ds(pl.multiple_of(place * tile_tok, width), window_rows), :]

    flag = (lax.axis_index("tm") == 0).astype(F32)
    kinds = table_ref.shape[0]
    label = jnp.concatenate([ref[...] for ref in labels], axis=1)
    kind = lax.broadcasted_iota(jnp.int32, (kinds, tokens), 0)
    one_hot = (jnp.broadcast_to(label, (kinds, tokens)) == kind).astype(F32)
    label_rows = dot_on(one_hot, table_ref[...], 0, 0, lax.Precision.HIGHEST)
    memory_ref[...] = (encoded.astype(F32) + flag * label_rows).astype(BF16)
    encoded_ref[...] = encoded
    loads[4].wait()
    loads[5].wait()


def state_body(
    share, first_head, encoded_ref, memory_ref, key_ref, value_ref, decay_ref, *out_refs
):
    state_ref, product_ref, pay_ref = out_refs
    heads = product_ref.shape[0]
    key_dim, val_dim = key_ref.shape[1] // share, value_ref.shape[1] // share
    tokens = encoded_ref.shape[0]
    cols = slice(first_head * key_dim, (first_head + heads) * key_dim)
    val_cols = slice(first_head * val_dim, (first_head + heads) * val_dim)
    keys = dot(encoded_ref[...], key_ref[:, cols]).astype(BF16)
    values = dot(memory_ref[...], value_ref[:, val_cols]).astype(BF16)
    states = []
    for h in range(heads):
        state = dot_on(
            keys[:, h * key_dim : (h + 1) * key_dim],
            values[:, h * val_dim : (h + 1) * val_dim],
            0,
            0,
        ) * tokens ** (-0.5)
        state_ref[h * key_dim : (h + 1) * key_dim, :] = state
        states.append(state)
    start = lax.axis_index("space") * share + first_head
    product = jnp.concatenate(
        [jnp.full((1, val_dim), decay_ref[0, start + h], F32) for h in range(heads)], axis=0
    )
    product_ref[...] = product
    write_payload(pay_ref, states, product, heads, key_dim)


def combine_body(bit, share, first, last, recv_ref, total_ref, product_ref, *refs):
    if first:
        rate_ref = product_ref
        outs = refs
    else:
        reach_ref, prefix_ref = refs[:2]
        outs = refs[2:]
    rows = total_ref.shape[0]
    key_dim = rows // share
    upper = (lax.axis_index("tm") >> bit) & 1
    is_upper = jnp.full(product_ref.shape, upper, jnp.int32) == 1
    product = product_ref[...]
    reach = product if first else reach_ref[...]
    tail = recv_ref[rows:, :].astype(F32)
    got = tail[:share] + tail[share : 2 * share] + tail[2 * share : 3 * share]
    ones = jnp.ones_like(product)
    on_got = jnp.where(is_upper, product, ones)
    on_own = jnp.where(is_upper, ones, got)
    on_prefix = jnp.where(is_upper, reach, jnp.zeros_like(product))
    totals = []
    for h in range(share):
        part = slice(h * key_dim, (h + 1) * key_dim)
        arrived = recv_ref[part, :].astype(F32)
        prefix = on_prefix[h : h + 1] * arrived
        if not first:
            prefix = prefix + prefix_ref[part, :]
        if last:
            outs[0][part, :] = prefix.astype(BF16)
        else:
            outs[3][part, :] = prefix
            total = on_got[h : h + 1] * arrived + on_own[h : h + 1] * total_ref[part, :]
            totals.append(total)
            outs[0][part, :] = total
    if not last:
        joined = product * got
        outs[1][...] = joined
        outs[2][...] = jnp.where(is_upper, reach * got, reach)
        write_payload(outs[4], totals, joined, share, key_dim)


def keys_body(window_ref, key_ref, out_ref):
    out_ref[...] = dot(window_ref[...], key_ref[...]).astype(BF16)


def decode_body(
    width, heads, key_ref, window_ref, memory_ref, read_ref, conv_ref, up_ref, spread_ref, out_ref
):
    rows, dim = window_ref.shape
    tile_tok = rows - 2 * width
    key_dim = key_ref.shape[1] // heads
    reads = [
        (
            dot(
                key_ref[:, h * key_dim : (h + 1) * key_dim],
                memory_ref[h * key_dim : (h + 1) * key_dim, :],
            )
            * key_dim ** (-0.5)
        ).astype(BF16)
        for h in range(heads)
    ]
    readout = jnp.concatenate(reads, axis=1)
    joined = (window_ref[...].astype(F32) + dot(readout, read_ref[...])).astype(BF16)
    columns = []
    for b in range(3):
        total = dot_on(joined[:tile_tok], conv_ref[0, b], 1, 1)
        for a in range(1, 3):
            total = total + dot_on(
                joined[a * width : a * width + tile_tok], conv_ref[a, b], 1, 1
            )
        columns.append(total)
    col = lax.broadcasted_iota(jnp.int32, columns[0].shape, 0) % width
    zero = jnp.zeros_like(columns[0])
    left = jnp.where(col == 0, zero, pltpu.roll(columns[0], 1, 0))
    right = jnp.where(col == width - 1, zero, pltpu.roll(columns[2], tile_tok - 1, 0))
    mapped = jax.nn.gelu(left + columns[1] + right).astype(BF16)
    wide = width * UP
    lane = lax.broadcasted_iota(jnp.int32, (UP, UP, wide), 2)
    sub = lax.broadcasted_iota(jnp.int32, (UP, UP, wide), 1)
    chosen = (lane % UP) == sub
    for i in range(tile_tok // width):
        hidden = dot(spread_ref[...], mapped[i * width : (i + 1) * width]).astype(BF16)
        pixels = dot_on(up_ref[...], hidden, 1, 1).reshape(UP, UP, wide)
        picked = jnp.sum(jnp.where(chosen, pixels, jnp.zeros_like(pixels)), axis=1)
        out_ref[i * UP : (i + 1) * UP, :] = picked


def shards(
    frames_feat,
    prompt_labels,
    label_table,
    enc_qkv,
    enc_out,
    norm_gain,
    key_proj,
    value_proj,
    read_proj,
    decay,
    dec_conv,
    dec_up,
):
    _, tile_rows, width, dim = frames_feat.shape
    tile_tok = tile_rows * width
    bands, frames = lax.axis_size("space"), lax.axis_size("tm")
    tokens = tile_tok * bands
    heads = decay.shape[1]
    share = heads // bands
    key_dim, val_dim = key_proj.shape[1] // heads, value_proj.shape[1] // heads
    window_rows = tile_tok + 2 * width
    sds = pltpu.VMEM

    flat = frames_feat.reshape(tile_tok, dim)
    labels = prompt_labels.reshape(1, tile_tok)
    if bands == 2:
        swap = [(0, 1), (1, 0)]
        tiles = [flat, lax.ppermute(flat, "space", swap)]
        marks = [labels, lax.ppermute(labels, "space", swap)]
    else:
        tiles = [lax.all_gather(flat, "space", axis=0, tiled=True)]
        marks = [lax.all_gather(labels, "space", axis=1, tiled=True)]

    token = np.arange(tokens)
    cell = (token // width // 2) * (width // 2) + token % width // 2
    pool = jnp.asarray((cell[None, :] == np.arange(tokens // 4)[:, None]) * 0.25, BF16)
    wide = np.arange(width * UP)
    spread = jnp.asarray((wide[:, None] // UP) == np.arange(width)[None, :], BF16)

    parts = len(tiles)
    window, encoded, memory_in, own_keys, own_values = call(
        functools.partial(encode_body, width, parts),
        (
            sds((window_rows, dim), BF16),
            sds((tokens, dim), BF16),
            sds((tokens, dim), BF16),
            sds((dim, share * key_dim), BF16),
            sds((dim, share * val_dim), BF16),
        ),
        (
            pltpu.VMEM((tokens + 2 * width, dim), BF16),
            pltpu.VMEM(tiles[0].shape, BF16),
            pltpu.VMEM(pool.shape, BF16),
            pltpu.VMEM(enc_qkv.shape, BF16),
            pltpu.VMEM(enc_out.shape, BF16),
            pltpu.SemaphoreType.DMA((6,)),
        ),
        [pl.ANY] + [pltpu.VMEM] * (2 * parts + 1) + [pl.ANY] * 5,
    )(
        *tiles,
        *marks,
        label_table,
        norm_gain.reshape(1, dim),
        pool,
        enc_qkv,
        enc_out,
        key_proj,
        value_proj,
    )
    chains = 2 if share % 2 == 0 else 1
    group = share // chains
    rows = group * key_dim
    pay = sds((rows + carry_rows(group), val_dim), BF16)
    state = sds((rows, val_dim), F32)
    small = sds((group, val_dim), F32)
    held = [
        call(
            functools.partial(state_body, share, chain * group),
            (state, small, pay),
            (),
            [pltpu.VMEM] * 4 + [pltpu.SMEM],
        )(encoded, memory_in, own_keys, own_values, decay)
        for chain in range(chains)
    ]
    key_rows = call(keys_body, sds((window_rows, heads * key_dim), BF16))(window, key_proj)
    held = [(total, product, (), payload) for total, product, payload in held]
    steps = (frames - 1).bit_length()
    memories = []
    for bit in range(steps):
        first, last = bit == 0, bit == steps - 1
        pairs = [(i, i ^ (1 << bit)) for i in range(frames) if i ^ (1 << bit) < frames]
        body = functools.partial(combine_body, bit, group, first, last)
        for chain, (total, product, carried, payload) in enumerate(held):
            arrived = lax.ppermute(payload, "tm", pairs)
            if last:
                memories.append(
                    call(body, sds((rows, val_dim), BF16))(arrived, total, product, *carried)
                )
            else:
                total, product, reach, prefix, payload = call(
                    body, (state, small, small, state, pay)
                )(arrived, total, product, *carried)
                held[chain] = (total, product, (reach, prefix), payload)
    memory = memories[0] if chains == 1 else jnp.concatenate(memories, axis=0)
    memory = lax.all_gather(memory, "space", axis=0, tiled=True)
    logits = call(
        functools.partial(decode_body, width, heads),
        jax.ShapeDtypeStruct((tile_rows * UP, width * UP), F32),
    )(key_rows, window, memory, read_proj, dec_conv.swapaxes(2, 3), dec_up.T, spread)
    return logits[None]


def solution(mesh):
    return jax.shard_map(
        shards,
        mesh=mesh,
        in_specs=(
            P("tm", "space", None, None),
            P("space", None),
            P(),
            P(),
            P(),
            P(),
            P(),
            P(),
            P(),
            P("tm", None),
            P(),
            P(),
        ),
        out_specs=P("tm", "space", None),
        check_vma=False,
    )
```

```python
import functools

import jax
import jax.numpy as jnp
import numpy as np
from jax import lax
from jax.experimental import pallas as pl
from jax.experimental.pallas import tpu as pltpu
from jax.sharding import PartitionSpec as P

ENC_HEADS = 8
UP = 4
LANES = 128
ON_CHIP = 1 << 18
EPSILON = 1e-06
F32 = jnp.float32
BF16 = jnp.bfloat16
VMEM = pl.BlockSpec(memory_space=pltpu.VMEM)


def dot(a, b):
    return jnp.dot(a, b, preferred_element_type=F32)


def dot_on(a, b, dim_a, dim_b, precision=None):
    return lax.dot_general(
        a, b, (((dim_a,), (dim_b,)), ((), ())), precision=precision, preferred_element_type=F32
    )


def call_in(chip, body, outs, scratch=(), spaces=None, micros=0):
    def result(x):
        shaped = jax.ShapeDtypeStruct(x.shape, x.dtype)
        return x if chip or isinstance(x, jax.ShapeDtypeStruct) else shaped

    outs = jax.tree.map(result, outs)

    def run(*operands):
        places = [pltpu.VMEM] * len(operands) if spaces is None else spaces
        kernel = pl.pallas_call(
            body,
            out_shape=outs,
            in_specs=[pl.BlockSpec(memory_space=place) for place in places],
            out_specs=jax.tree.map(lambda _: VMEM, outs),
            scratch_shapes=scratch,
            cost_estimate=pl.CostEstimate(
                flops=int(micros * 1e9), transcendentals=0, bytes_accessed=0
            ),
        )
        held = chip and pltpu.VMEM
        return kernel(
            *[
                pltpu.with_memory_space_constraint(x, place) if place is held else x
                for x, place in zip(operands, places)
            ]
        )

    return run


def carry_rows(share):
    return -(-3 * share // 16) * 16


def split(x):
    high = x.astype(BF16).astype(F32)
    mid = (x - high).astype(BF16).astype(F32)
    low = (x - high - mid).astype(BF16).astype(F32)
    return [high, mid, low]


def write_payload(pay_ref, totals, product, share, key_dim):
    for h in range(share):
        rows = slice(h * key_dim, (h + 1) * key_dim)
        pay_ref[rows, :] = totals[h].astype(BF16)
    parts = split(product)
    tail = carry_rows(share)
    if tail > 3 * share:
        parts.append(jnp.zeros((tail - 3 * share, product.shape[1]), F32))
    pay_ref[share * key_dim :, :] = jnp.concatenate(parts, axis=0).astype(BF16)


def project_body(loaded, *refs):
    sources, targets = refs[:loaded], refs[loaded : 2 * loaded]
    query_ref, pair_ref, sems = refs[2 * loaded :]
    tile_ref, pool_ref, qkv_ref = targets[:3]
    dim = tile_ref.shape[1]
    loads = [
        pltpu.make_async_copy(source, target, sems.at[n])
        for n, (source, target) in enumerate(zip(sources, targets))
    ]
    for load in loads:
        load.start()
    loads[0].wait()
    loads[1].wait()
    pooled = dot(pool_ref[...], tile_ref[...]).astype(BF16)
    loads[2].wait()
    pair_ref[...] = dot(pooled, qkv_ref[:, dim:]).astype(BF16)
    query_ref[...] = dot(tile_ref[...], qkv_ref[:, :dim]).astype(BF16)
    for load in loads[3:]:
        load.wait()


def encode_body(width, parts, *refs):
    tiles, labels = refs[:parts], refs[parts : 2 * parts]
    rest = refs[2 * parts :]
    query_ref, pair_ref, pool_ref, qkv_ref, table_ref, gain_ref, out_ref, key_ref = rest[:8]
    window_ref, encoded_ref, memory_ref, turned_ref, padded = rest[8:]
    place = lax.axis_index("space")
    dim = query_ref.shape[1]
    size = dim // ENC_HEADS
    window_rows = window_ref.shape[0]
    tile_tok = window_rows - 2 * width
    queries, pairs = [query_ref[...]], [pair_ref[...]]
    for tile in tiles[1:]:
        queries.append(dot(tile[...], qkv_ref[:, :dim]).astype(BF16))
        pooled = dot(pool_ref[...], tile[...]).astype(BF16)
        pairs.append(dot(pooled, qkv_ref[:, dim:]).astype(BF16))
    x = jnp.concatenate([tile[...] for tile in tiles], axis=0)
    queries = jnp.concatenate(queries, axis=0)
    pair = jnp.concatenate(pairs, axis=0)
    tokens = x.shape[0]
    count = pair.shape[0]
    lane = lax.broadcasted_iota(jnp.int32, (count, dim), 1)
    masks = [(lane >= h * size) & (lane < (h + 1) * size) for h in range(ENC_HEADS)]
    zero = jnp.zeros((count, dim), BF16)
    keys = jnp.concatenate([jnp.where(m, pair[:, :dim], zero) for m in masks], axis=0)
    values = jnp.concatenate([jnp.where(m, pair[:, dim:], zero) for m in masks], axis=0)
    scores = (dot_on(keys, queries, 1, 1) * size ** (-0.5)).reshape(ENC_HEADS, count, tokens)
    weights = jnp.exp(scores - jnp.max(scores, axis=1, keepdims=True))
    totals = jnp.sum(weights, axis=1, keepdims=True)
    rounded = weights.astype(BF16).reshape(ENC_HEADS * count, tokens)
    summed = dot_on(values, rounded, 0, 0).reshape(ENC_HEADS, size, tokens)
    attended = (summed / totals).reshape(dim, tokens).astype(BF16)
    hidden = x.astype(F32) + dot_on(attended, out_ref[...], 0, 0)
    scale = lax.rsqrt(jnp.mean(hidden * hidden, axis=-1, keepdims=True) + EPSILON)
    encoded = (hidden * scale * gain_ref[...]).astype(BF16)
    encoded_ref[...] = encoded

    flag = (lax.axis_index("tm") == 0).astype(F32)
    kinds = table_ref.shape[0]
    label = jnp.concatenate(
        [ref[r : r + 1, :] for ref in labels for r in range(ref.shape[0])], axis=1
    )
    kind = lax.broadcasted_iota(jnp.int32, (kinds, tokens), 0)
    one_hot = (jnp.broadcast_to(label, (kinds, tokens)) == kind).astype(F32)
    one_hot = jnp.concatenate([one_hot] * 3, axis=0).astype(BF16)
    label_rows = dot_on(one_hot, jnp.concatenate(split(table_ref[...]), axis=0).astype(BF16), 0, 0)
    memory_ref[...] = (encoded.astype(F32) + flag * label_rows).astype(BF16)

    edge = jnp.zeros((width, dim), BF16)
    padded[:width, :] = edge
    padded[width + tokens :, :] = edge
    for p in range(parts):
        spot = place if p == 0 else 1 - place
        spot = pl.multiple_of(width + spot * tile_tok, width) if parts > 1 else width
        rows = tokens // parts
        padded[pl.ds(spot, rows), :] = encoded[p * rows : (p + 1) * rows]
    window_ref[...] = padded[pl.ds(pl.multiple_of(place * tile_tok, width), window_rows), :]
    cols = turned_ref.shape[0]
    turned_ref[...] = key_ref[:, pl.ds(pl.multiple_of(place * cols, LANES), cols)].T


def state_body(
    share, first_head, encoded_ref, memory_ref, turned_ref, value_ref, decay_ref, *out_refs
):
    state_ref, product_ref, pay_ref = out_refs
    heads = product_ref.shape[0]
    key_dim = turned_ref.shape[0] // share
    val_dim = state_ref.shape[1]
    tokens = encoded_ref.shape[0]
    cols = slice(first_head * key_dim, (first_head + heads) * key_dim)
    start = lax.axis_index("space") * share + first_head
    val_cols = pl.ds(pl.multiple_of(start * val_dim, val_dim), heads * val_dim)
    keys = dot_on(turned_ref[cols, :], encoded_ref[...], 1, 1).astype(BF16)
    values = dot(memory_ref[...], value_ref[:, val_cols]).astype(BF16)
    states = []
    for h in range(heads):
        state = dot(
            keys[h * key_dim : (h + 1) * key_dim], values[:, h * val_dim : (h + 1) * val_dim]
        ) * tokens ** (-0.5)
        state_ref[h * key_dim : (h + 1) * key_dim, :] = state
        states.append(state)
    rates = jnp.broadcast_to(decay_ref[...], (heads, decay_ref.shape[1]))
    head = lax.broadcasted_iota(jnp.int32, rates.shape, 0) + start
    picked = lax.broadcasted_iota(jnp.int32, rates.shape, 1) == head
    rate = jnp.sum(jnp.where(picked, rates, jnp.zeros_like(rates)), axis=1, keepdims=True)
    product = jnp.broadcast_to(rate, (heads, val_dim))
    product_ref[...] = product
    write_payload(pay_ref, states, product, heads, key_dim)


def combine_body(bit, share, first, last, recv_ref, total_ref, product_ref, *refs):
    if not first:
        reach_ref, prefix_ref = refs[:2]
    outs = refs[-1:] if last else refs[-5:]
    rows = total_ref.shape[0]
    key_dim = rows // share
    upper = (lax.axis_index("tm") >> bit) & 1
    is_upper = jnp.full(product_ref.shape, upper, jnp.int32) == 1
    product = product_ref[...]
    reach = product if first else reach_ref[...]
    tail = recv_ref[rows:, :].astype(F32)
    got = tail[:share] + tail[share : 2 * share] + tail[2 * share : 3 * share]
    ones = jnp.ones_like(product)
    on_got = jnp.where(is_upper, product, ones)
    on_own = jnp.where(is_upper, ones, got)
    on_prefix = jnp.where(is_upper, reach, jnp.zeros_like(product))
    totals = []
    for h in range(share):
        part = slice(h * key_dim, (h + 1) * key_dim)
        arrived = recv_ref[part, :].astype(F32)
        prefix = on_prefix[h : h + 1] * arrived
        if not first:
            prefix = prefix + prefix_ref[part, :]
        if last:
            outs[0][part, :] = prefix.astype(BF16)
        else:
            outs[3][part, :] = prefix
            total = on_got[h : h + 1] * arrived + on_own[h : h + 1] * total_ref[part, :]
            totals.append(total)
            outs[0][part, :] = total
    if not last:
        joined = product * got
        outs[1][...] = joined
        outs[2][...] = jnp.where(is_upper, reach * got, reach)
        write_payload(outs[4], totals, joined, share, key_dim)


def keys_body(window_ref, after, key_hbm, *refs):
    count = (len(refs) - 3) // 2
    sources, out_ref, targets, (key_ref, sems) = (
        refs[:count],
        refs[count],
        refs[count + 1 : -2],
        refs[-2:],
    )
    loads = [
        pltpu.make_async_copy(source, target, sems.at[n])
        for n, (source, target) in enumerate(zip((key_hbm, *sources), (key_ref, *targets)))
    ]
    for load in loads:
        load.start()
    loads[0].wait()
    out_ref[...] = dot(window_ref[...], key_ref[...]).astype(BF16)
    for load in loads[1:]:
        load.wait()


def read_rows(heads, firsts, key_ref, read_ref, memories):
    key_dim = key_ref.shape[1] // heads
    total = None
    for first, memory_ref in zip(firsts, memories):
        count = memory_ref.shape[0] // key_dim
        start = first * key_dim
        start = start if isinstance(start, int) else pl.multiple_of(start, key_dim)
        keys = key_ref[:, pl.ds(start, count * key_dim)]
        reads = [
            dot(
                keys[:, h * key_dim : (h + 1) * key_dim],
                memory_ref[h * key_dim : (h + 1) * key_dim, :],
            )
            * key_dim ** (-0.5)
            for h in range(count)
        ]
        val_dim = memory_ref.shape[1]
        start = first * val_dim
        start = start if isinstance(start, int) else pl.multiple_of(start, val_dim)
        readout = jnp.concatenate(reads, axis=1).astype(BF16)
        piece = dot(readout, read_ref[pl.ds(start, count * val_dim), :])
        total = piece if total is None else total + piece
    return total


def own_first(share, offset, flip):
    place = lax.axis_index("space")
    return [(1 - place if flip else place) * share + offset]


def read_body(heads, firsts, begun, *refs):
    out_ref = refs[-1]
    key_ref, read_ref = refs[:2]
    memories = refs[2 + begun : -1]
    total = read_rows(heads, firsts(), key_ref, read_ref, memories)
    out_ref[...] = refs[2][...] + total if begun else total


def decode_body(width, heads, firsts, key_ref, read_ref, begun_ref, *refs):
    memories = refs[:-5]
    window_ref, conv_ref, up_ref, spread_ref, out_ref = refs[-5:]
    rows = window_ref.shape[0]
    tile_tok = rows - 2 * width
    total = read_rows(heads, firsts(), key_ref, read_ref, memories) + begun_ref[...]
    joined = (window_ref[...].astype(F32) + total).astype(BF16)
    summed = dot_on(joined[:tile_tok], conv_ref[0], 1, 1)
    for a in range(1, 3):
        summed = summed + dot_on(joined[a * width : a * width + tile_tok], conv_ref[a], 1, 1)
    chans = summed.shape[1] // 3
    columns = [summed[:, b * chans : (b + 1) * chans] for b in range(3)]
    col = lax.broadcasted_iota(jnp.int32, columns[0].shape, 0) % width
    zero = jnp.zeros_like(columns[0])
    left = jnp.where(col == 0, zero, pltpu.roll(columns[0], 1, 0))
    right = jnp.where(col == width - 1, zero, pltpu.roll(columns[2], tile_tok - 1, 0))
    mapped = jax.nn.gelu(left + columns[1] + right).astype(BF16)
    wide = tile_tok * UP
    lane = lax.broadcasted_iota(jnp.int32, (UP, UP, wide), 2)
    sub = lax.broadcasted_iota(jnp.int32, (UP, UP, wide), 1)
    hidden = dot(spread_ref[...], mapped).astype(BF16)
    pixels = dot_on(up_ref[...], hidden, 1, 1).reshape(UP, UP, wide)
    picked = jnp.sum(jnp.where((lane % UP) == sub, pixels, jnp.zeros_like(pixels)), axis=1)
    line = width * UP
    for i in range(tile_tok // width):
        out_ref[i * UP : (i + 1) * UP, :] = picked[:, i * line : (i + 1) * line]


def shards(
    frames_feat,
    prompt_labels,
    label_table,
    enc_qkv,
    enc_out,
    norm_gain,
    key_proj,
    value_proj,
    read_proj,
    decay,
    dec_conv,
    dec_up,
):
    _, tile_rows, width, dim = frames_feat.shape
    tile_tok = tile_rows * width
    bands, frames = lax.axis_size("space"), lax.axis_size("tm")
    tokens = tile_tok * bands
    heads = decay.shape[1]
    share = heads // bands
    key_dim, val_dim = key_proj.shape[1] // heads, value_proj.shape[1] // heads
    window_rows = tile_tok + 2 * width
    sds = pltpu.VMEM
    call = functools.partial(call_in, 2 * tokens * dim <= ON_CHIP)

    flat = frames_feat.reshape(tile_tok, dim)
    swap = [(0, 1), (1, 0)]
    if bands == 2:
        tiles = [flat, lax.ppermute(flat, "space", swap)]
        marks = [prompt_labels, lax.ppermute(prompt_labels, "space", swap)]
    else:
        tiles = [lax.all_gather(flat, "space", axis=0, tiled=True)]
        marks = [lax.all_gather(prompt_labels, "space", axis=0, tiled=True)]
    parts = len(tiles)
    tile = tiles[0].shape

    token = np.arange(tile[0])
    cell = (token // width // 2) * (width // 2) + token % width // 2
    pool = jnp.asarray((cell[None, :] == np.arange(tile[0] // 4)[:, None]) * 0.25, BF16)
    wide = np.arange(tile_tok * UP)
    row = wide // (width * UP) * width + wide % (width * UP) // UP
    spread = jnp.asarray(row[:, None] == np.arange(tile_tok)[None, :], BF16)

    gain = norm_gain.reshape(1, dim)
    loaded = [tiles[0], pool, enc_qkv, marks[0], label_table, gain, decay]
    tiles[0], pool, qkv, marks[0], table, gain, rates, queries, pairs = call(
        functools.partial(project_body, len(loaded)),
        (
            *[sds(x.shape, x.dtype) for x in loaded],
            sds(tile, BF16),
            sds((tile[0] // 4, 2 * dim), BF16),
        ),
        (pltpu.SemaphoreType.DMA((len(loaded),)),),
        [pl.ANY] * len(loaded),
        micros=1,
    )(*loaded)
    window, encoded, memory_in, turned = call(
        functools.partial(encode_body, width, parts),
        (
            sds((window_rows, dim), BF16),
            sds((tokens, dim), BF16),
            sds((tokens, dim), BF16),
            sds((share * key_dim, dim), BF16),
        ),
        (pltpu.VMEM((tokens + 2 * width, dim), BF16),),
        micros=2,
    )(
        *tiles,
        *marks,
        queries,
        pairs,
        pool,
        qkv,
        table,
        gain,
        enc_out,
        key_proj,
    )
    chains = 2 if share % 2 == 0 else 1
    group = share // chains
    rows = group * key_dim
    pay = sds((rows + carry_rows(group), val_dim), BF16)
    state = sds((rows, val_dim), F32)
    small = sds((group, val_dim), F32)
    held = [
        call(
            functools.partial(state_body, share, chain * group),
            (state, small, pay),
        )(encoded, memory_in, turned, value_proj, rates)
        for chain in range(chains)
    ]
    conv = dec_conv.swapaxes(2, 3)
    late = [read_proj, conv.reshape(conv.shape[0], -1, conv.shape[3]), dec_up.T, spread]
    held = [(total, product, (), payload) for total, product, payload in held]
    steps = (frames - 1).bit_length()
    for bit in range(steps):
        first, last = bit == 0, bit == steps - 1
        pairs = [(i, i ^ (1 << bit)) for i in range(frames) if i ^ (1 << bit) < frames]
        body = functools.partial(combine_body, bit, group, first, last)
        for chain, (total, product, carried, payload) in enumerate(held):
            arrived = lax.ppermute(payload, "tm", pairs)
            if last:
                held[chain] = (arrived, total, product, *carried)
                ahead = payload
            else:
                total, product, reach, prefix, payload = call(
                    body, (state, small, small, state, pay)
                )(arrived, total, product, *carried)
                held[chain] = (total, product, (reach, prefix), payload)

    key_rows, *late = call(
        keys_body,
        (sds((window_rows, heads * key_dim), BF16), *[sds(x.shape, BF16) for x in late]),
        (pltpu.VMEM(key_proj.shape, BF16), pltpu.SemaphoreType.DMA((5,))),
        [pltpu.VMEM] * 2 + [pl.ANY] * (1 + len(late)),
    )(window, ahead, key_proj, *late)
    read_out, *late = late

    def read(firsts, arrays, begun):
        body = functools.partial(read_body, heads, firsts, len(begun))
        return [call(body, sds((window_rows, dim), F32))(key_rows, read_out, *begun, *arrays)]

    order, begun, pieces = key_rows, [], []
    for chain, operands in enumerate(held):
        memory = call(body, sds((rows, val_dim), BF16))(*operands, order)
        offset = chain * group
        if bands == 2:
            pieces.append((functools.partial(own_first, share, offset, False), [memory]))
            other = lax.ppermute(memory, "space", swap)
            pieces.append((functools.partial(own_first, share, offset, True), [other]))
        else:
            every = lax.all_gather(memory, "space", axis=0)
            firsts = [band * share + offset for band in range(bands)]
            pieces.append((lambda firsts=firsts: firsts, [every[band] for band in range(bands)]))
        if chain < chains - 1:
            begun = read(*pieces.pop(0), begun)
            order = begun[0]
    for piece in pieces[:-1]:
        begun = read(*piece, begun)
    if not begun:
        begun = [jnp.zeros((window_rows, dim), F32)]
    firsts, arrays = pieces[-1]
    logits = call(
        functools.partial(decode_body, width, heads, firsts),
        jax.ShapeDtypeStruct((tile_rows * UP, width * UP), F32),
    )(key_rows, read_out, *begun, *arrays, window, *late)
    return logits[None]


def solution(mesh):
    return jax.shard_map(
        shards,
        mesh=mesh,
        in_specs=(
            P("tm", "space", None, None),
            P("space", None),
            P(),
            P(),
            P(),
            P(),
            P(),
            P(),
            P(),
            P("tm", None),
            P(),
            P(),
        ),
        out_specs=P("tm", "space", None),
        check_vma=False,
    )
```

```python
import functools

import jax
import jax.numpy as jnp
import numpy as np
from jax import lax
from jax.experimental import pallas as pl
from jax.experimental.pallas import tpu as pltpu
from jax.sharding import PartitionSpec as P

ENC_HEADS = 8
UP = 4
LANES = 128
ON_CHIP = 1 << 18
SIZES = [2, 2]
CROSSED_BITS = 1
EPSILON = 1e-06
F32 = jnp.float32
BF16 = jnp.bfloat16
VMEM = pl.BlockSpec(memory_space=pltpu.VMEM)


def dot(a, b):
    return jnp.dot(a, b, preferred_element_type=F32)


def dot_on(a, b, dim_a, dim_b, precision=None):
    return lax.dot_general(
        a, b, (((dim_a,), (dim_b,)), ((), ())), precision=precision, preferred_element_type=F32
    )


def call_in(chip, body, outs, scratch=(), spaces=None, micros=0):
    def result(x):
        shaped = jax.ShapeDtypeStruct(x.shape, x.dtype)
        return x if chip or isinstance(x, jax.ShapeDtypeStruct) else shaped

    outs = jax.tree.map(result, outs)

    def run(*operands):
        places = [pltpu.VMEM] * len(operands) if spaces is None else spaces
        kernel = pl.pallas_call(
            body,
            out_shape=outs,
            in_specs=[pl.BlockSpec(memory_space=place) for place in places],
            out_specs=jax.tree.map(lambda _: VMEM, outs),
            scratch_shapes=scratch,
            cost_estimate=pl.CostEstimate(
                flops=int(micros * 1e9), transcendentals=0, bytes_accessed=0
            ),
        )
        held = chip and pltpu.VMEM
        return kernel(
            *[
                pltpu.with_memory_space_constraint(x, place) if place is held else x
                for x, place in zip(operands, places)
            ]
        )

    return run


def own_band(crossed):
    band = lax.axis_index("space")
    if crossed:
        bits = lax.axis_index("tm") & CROSSED_BITS
        shift = 16
        while shift:
            bits = bits ^ (bits >> shift)
            shift //= 2
        band = (band + bits) & 1
    return band


def carry_rows(share):
    return -(-3 * share // 16) * 16


def split(x):
    high = x.astype(BF16).astype(F32)
    mid = (x - high).astype(BF16).astype(F32)
    low = (x - high - mid).astype(BF16).astype(F32)
    return [high, mid, low]


def write_payload(pay_ref, totals, product, share, key_dim):
    for h in range(share):
        rows = slice(h * key_dim, (h + 1) * key_dim)
        pay_ref[rows, :] = totals[h].astype(BF16)
    tail = pay_ref.shape[0] - share * key_dim
    if tail == 0:
        return
    parts = split(product)
    if tail > 3 * share:
        parts.append(jnp.zeros((tail - 3 * share, product.shape[1]), F32))
    pay_ref[share * key_dim :, :] = jnp.concatenate(parts, axis=0).astype(BF16)


def project_body(loaded, *refs):
    sources, targets = refs[:loaded], refs[loaded : 2 * loaded]
    query_ref, pair_ref, sems = refs[2 * loaded :]
    tile_ref, pool_ref, qkv_ref = targets[:3]
    dim = tile_ref.shape[1]
    loads = [
        pltpu.make_async_copy(source, target, sems.at[n])
        for n, (source, target) in enumerate(zip(sources, targets))
    ]
    for load in loads:
        load.start()
    loads[0].wait()
    loads[1].wait()
    pooled = dot(pool_ref[...], tile_ref[...]).astype(BF16)
    loads[2].wait()
    pair_ref[...] = dot(pooled, qkv_ref[:, dim:]).astype(BF16)
    query_ref[...] = dot(tile_ref[...], qkv_ref[:, :dim]).astype(BF16)
    for load in loads[3:]:
        load.wait()


def encode_body(width, parts, *refs):
    tiles, labels = refs[:parts], refs[parts : 2 * parts]
    rest = refs[2 * parts :]
    query_ref, pair_ref, pool_ref, qkv_ref, table_ref, gain_ref, out_ref, key_ref = rest[:8]
    window_ref, encoded_ref, memory_ref, turned_ref, padded = rest[8:]
    place = lax.axis_index("space")
    dim = query_ref.shape[1]
    size = dim // ENC_HEADS
    window_rows = window_ref.shape[0]
    tile_tok = window_rows - 2 * width
    queries, pairs = [query_ref[...]], [pair_ref[...]]
    for tile in tiles[1:]:
        queries.append(dot(tile[...], qkv_ref[:, :dim]).astype(BF16))
        pooled = dot(pool_ref[...], tile[...]).astype(BF16)
        pairs.append(dot(pooled, qkv_ref[:, dim:]).astype(BF16))
    x = jnp.concatenate([tile[...] for tile in tiles], axis=0)
    queries = jnp.concatenate(queries, axis=0)
    pair = jnp.concatenate(pairs, axis=0)
    tokens = x.shape[0]
    count = pair.shape[0]
    lane = lax.broadcasted_iota(jnp.int32, (count, dim), 1)
    masks = [(lane >= h * size) & (lane < (h + 1) * size) for h in range(ENC_HEADS)]
    zero = jnp.zeros((count, dim), BF16)
    keys = jnp.concatenate([jnp.where(m, pair[:, :dim], zero) for m in masks], axis=0)
    values = jnp.concatenate([jnp.where(m, pair[:, dim:], zero) for m in masks], axis=0)
    scores = (dot_on(keys, queries, 1, 1) * size ** (-0.5)).reshape(ENC_HEADS, count, tokens)
    weights = jnp.exp(scores - jnp.max(scores, axis=1, keepdims=True))
    totals = jnp.sum(weights, axis=1, keepdims=True)
    rounded = weights.astype(BF16).reshape(ENC_HEADS * count, tokens)
    summed = dot_on(values, rounded, 0, 0).reshape(ENC_HEADS, size, tokens)
    attended = (summed / totals).reshape(dim, tokens).astype(BF16)
    hidden = x.astype(F32) + dot_on(attended, out_ref[...], 0, 0)
    scale = lax.rsqrt(jnp.mean(hidden * hidden, axis=-1, keepdims=True) + EPSILON)
    encoded = (hidden * scale * gain_ref[...]).astype(BF16)
    encoded_ref[...] = encoded

    flag = (lax.axis_index("tm") == 0).astype(F32)
    kinds = table_ref.shape[0]
    label = jnp.concatenate(
        [ref[r : r + 1, :] for ref in labels for r in range(ref.shape[0])], axis=1
    )
    kind = lax.broadcasted_iota(jnp.int32, (kinds, tokens), 0)
    one_hot = (jnp.broadcast_to(label, (kinds, tokens)) == kind).astype(F32)
    one_hot = jnp.concatenate([one_hot] * 3, axis=0).astype(BF16)
    label_rows = dot_on(one_hot, jnp.concatenate(split(table_ref[...]), axis=0).astype(BF16), 0, 0)
    memory_ref[...] = (encoded.astype(F32) + flag * label_rows).astype(BF16)

    edge = jnp.zeros((width, dim), BF16)
    padded[:width, :] = edge
    padded[width + tokens :, :] = edge
    for p in range(parts):
        spot = place if p == 0 else 1 - place
        spot = pl.multiple_of(width + spot * tile_tok, width) if parts > 1 else width
        rows = tokens // parts
        padded[pl.ds(spot, rows), :] = encoded[p * rows : (p + 1) * rows]
    window_ref[...] = padded[pl.ds(pl.multiple_of(place * tile_tok, width), window_rows), :]
    cols = turned_ref.shape[0]
    start = pl.multiple_of(own_band(parts == 2) * cols, LANES)
    turned_ref[...] = key_ref[:, pl.ds(start, cols)].T


def state_body(
    share, crossed, first_head, encoded_ref, memory_ref, turned_ref, value_ref, decay_ref, *out_refs
):
    state_ref, product_ref, pay_ref = out_refs
    heads = product_ref.shape[0]
    key_dim = turned_ref.shape[0] // share
    val_dim = state_ref.shape[1]
    tokens = encoded_ref.shape[0]
    cols = slice(first_head * key_dim, (first_head + heads) * key_dim)
    start = own_band(crossed) * share + first_head
    val_cols = pl.ds(pl.multiple_of(start * val_dim, val_dim), heads * val_dim)
    keys = dot_on(turned_ref[cols, :], encoded_ref[...], 1, 1).astype(BF16)
    values = dot(memory_ref[...], value_ref[:, val_cols]).astype(BF16)
    states = []
    for h in range(heads):
        state = dot(
            keys[h * key_dim : (h + 1) * key_dim], values[:, h * val_dim : (h + 1) * val_dim]
        ) * tokens ** (-0.5)
        state_ref[h * key_dim : (h + 1) * key_dim, :] = state
        states.append(state)
    rates = jnp.broadcast_to(decay_ref[...], (heads, decay_ref.shape[1]))
    head = lax.broadcasted_iota(jnp.int32, rates.shape, 0) + start
    picked = lax.broadcasted_iota(jnp.int32, rates.shape, 1) == head
    rate = jnp.sum(jnp.where(picked, rates, jnp.zeros_like(rates)), axis=1, keepdims=True)
    product = jnp.broadcast_to(rate, (heads, val_dim))
    product_ref[...] = product
    write_payload(pay_ref, states, product, heads, key_dim)


def combine_body(bit, share, first, last, recv_ref, total_ref, product_ref, *refs):
    if not first:
        reach_ref, prefix_ref = refs[:2]
    outs = refs[-1:] if last else refs[-5:]
    rows = total_ref.shape[0]
    key_dim = rows // share
    upper = (lax.axis_index("tm") >> bit) & 1
    is_upper = jnp.full(product_ref.shape, upper, jnp.int32) == 1
    product = product_ref[...]
    reach = product if first else reach_ref[...]
    if not last:
        tail = recv_ref[rows:, :].astype(F32)
        got = tail[:share] + tail[share : 2 * share] + tail[2 * share : 3 * share]
        ones = jnp.ones_like(product)
        on_got = jnp.where(is_upper, product, ones)
        on_own = jnp.where(is_upper, ones, got)
    on_prefix = jnp.where(is_upper, reach, jnp.zeros_like(product))
    totals = []
    for h in range(share):
        part = slice(h * key_dim, (h + 1) * key_dim)
        arrived = recv_ref[part, :].astype(F32)
        prefix = on_prefix[h : h + 1] * arrived
        if not first:
            prefix = prefix + prefix_ref[part, :]
        if last:
            outs[0][part, :] = prefix.astype(BF16)
        else:
            outs[3][part, :] = prefix
            total = on_got[h : h + 1] * arrived + on_own[h : h + 1] * total_ref[part, :]
            totals.append(total)
            outs[0][part, :] = total
    if not last:
        joined = product * got
        outs[1][...] = joined
        outs[2][...] = jnp.where(is_upper, reach * got, reach)
        write_payload(outs[4], totals, joined, share, key_dim)


def keys_body(window_ref, after, key_hbm, *refs):
    count = (len(refs) - 3) // 2
    sources, out_ref, targets, (key_ref, sems) = (
        refs[:count],
        refs[count],
        refs[count + 1 : -2],
        refs[-2:],
    )
    loads = [
        pltpu.make_async_copy(source, target, sems.at[n])
        for n, (source, target) in enumerate(zip((key_hbm, *sources), (key_ref, *targets)))
    ]
    for load in loads:
        load.start()
    loads[0].wait()
    out_ref[...] = dot(window_ref[...], key_ref[...]).astype(BF16)
    for load in loads[1:]:
        load.wait()


def read_rows(heads, firsts, key_ref, read_ref, memories):
    key_dim = key_ref.shape[1] // heads
    total = None
    for first, memory_ref in zip(firsts, memories):
        count = memory_ref.shape[0] // key_dim
        start = first * key_dim
        start = start if isinstance(start, int) else pl.multiple_of(start, key_dim)
        keys = key_ref[:, pl.ds(start, count * key_dim)]
        reads = [
            dot(
                keys[:, h * key_dim : (h + 1) * key_dim],
                memory_ref[h * key_dim : (h + 1) * key_dim, :],
            )
            * key_dim ** (-0.5)
            for h in range(count)
        ]
        val_dim = memory_ref.shape[1]
        start = first * val_dim
        start = start if isinstance(start, int) else pl.multiple_of(start, val_dim)
        readout = jnp.concatenate(reads, axis=1).astype(BF16)
        piece = dot(readout, read_ref[pl.ds(start, count * val_dim), :])
        total = piece if total is None else total + piece
    return total


def own_first(share, offset, flip):
    place = own_band(True)
    return [(1 - place if flip else place) * share + offset]


def read_body(heads, firsts, begun, *refs):
    out_ref = refs[-1]
    key_ref, read_ref = refs[:2]
    memories = refs[2 + begun : -1]
    total = read_rows(heads, firsts(), key_ref, read_ref, memories)
    out_ref[...] = refs[2][...] + total if begun else total


def decode_body(width, heads, firsts, key_ref, read_ref, begun_ref, *refs):
    memories = refs[:-5]
    window_ref, conv_ref, up_ref, spread_ref, out_ref = refs[-5:]
    rows = window_ref.shape[0]
    tile_tok = rows - 2 * width
    total = read_rows(heads, firsts(), key_ref, read_ref, memories) + begun_ref[...]
    joined = (window_ref[...].astype(F32) + total).astype(BF16)
    summed = dot_on(joined[:tile_tok], conv_ref[0], 1, 1)
    for a in range(1, 3):
        summed = summed + dot_on(joined[a * width : a * width + tile_tok], conv_ref[a], 1, 1)
    chans = summed.shape[1] // 3
    columns = [summed[:, b * chans : (b + 1) * chans] for b in range(3)]
    col = lax.broadcasted_iota(jnp.int32, columns[0].shape, 0) % width
    zero = jnp.zeros_like(columns[0])
    left = jnp.where(col == 0, zero, pltpu.roll(columns[0], 1, 0))
    right = jnp.where(col == width - 1, zero, pltpu.roll(columns[2], tile_tok - 1, 0))
    mapped = jax.nn.gelu(left + columns[1] + right).astype(BF16)
    wide = tile_tok * UP
    lane = lax.broadcasted_iota(jnp.int32, (UP, UP, wide), 2)
    sub = lax.broadcasted_iota(jnp.int32, (UP, UP, wide), 1)
    small = jnp.concatenate(split(dot_on(up_ref[...], mapped, 1, 1)), axis=0).astype(BF16)
    parts = dot(small, spread_ref[...]).reshape(3, UP, UP, wide)
    pixels = parts[0] + parts[1] + parts[2]
    picked = jnp.sum(jnp.where((lane % UP) == sub, pixels, jnp.zeros_like(pixels)), axis=1)
    line = width * UP
    for i in range(tile_tok // width):
        out_ref[i * UP : (i + 1) * UP, :] = picked[:, i * line : (i + 1) * line]


def shards(
    frames_feat,
    prompt_labels,
    label_table,
    enc_qkv,
    enc_out,
    norm_gain,
    key_proj,
    value_proj,
    read_proj,
    decay,
    dec_conv,
    dec_up,
):
    _, tile_rows, width, dim = frames_feat.shape
    tile_tok = tile_rows * width
    bands, frames = lax.axis_size("space"), lax.axis_size("tm")
    tokens = tile_tok * bands
    heads = decay.shape[1]
    share = heads // bands
    key_dim, val_dim = key_proj.shape[1] // heads, value_proj.shape[1] // heads
    window_rows = tile_tok + 2 * width
    sds = pltpu.VMEM
    call = functools.partial(call_in, 2 * tokens * dim <= ON_CHIP)

    flat = frames_feat.reshape(tile_tok, dim)
    swap = [(0, 1), (1, 0)]
    if bands == 2:
        tiles = [flat, lax.ppermute(flat, "space", swap)]
        marks = [prompt_labels, lax.ppermute(prompt_labels, "space", swap)]
    else:
        tiles = [lax.all_gather(flat, "space", axis=0, tiled=True)]
        marks = [lax.all_gather(prompt_labels, "space", axis=0, tiled=True)]
    parts = len(tiles)
    tile = tiles[0].shape

    token = np.arange(tile[0])
    cell = (token // width // 2) * (width // 2) + token % width // 2
    pool = jnp.asarray((cell[None, :] == np.arange(tile[0] // 4)[:, None]) * 0.25, BF16)
    wide = np.arange(tile_tok * UP)
    row = wide // (width * UP) * width + wide % (width * UP) // UP
    spread = jnp.asarray(row[None, :] == np.arange(tile_tok)[:, None], BF16)

    gain = norm_gain.reshape(1, dim)
    loaded = [tiles[0], pool, enc_qkv, marks[0], label_table, gain, decay]
    tiles[0], pool, qkv, marks[0], table, gain, rates, queries, pairs = call(
        functools.partial(project_body, len(loaded)),
        (
            *[sds(x.shape, x.dtype) for x in loaded],
            sds(tile, BF16),
            sds((tile[0] // 4, 2 * dim), BF16),
        ),
        (pltpu.SemaphoreType.DMA((len(loaded),)),),
        [pl.ANY] * len(loaded),
        micros=1,
    )(*loaded)
    window, encoded, memory_in, turned = call(
        functools.partial(encode_body, width, parts),
        (
            sds((window_rows, dim), BF16),
            sds((tokens, dim), BF16),
            sds((tokens, dim), BF16),
            sds((share * key_dim, dim), BF16),
        ),
        (pltpu.VMEM((tokens + 2 * width, dim), BF16),),
        micros=2,
    )(
        *tiles,
        *marks,
        queries,
        pairs,
        pool,
        qkv,
        table,
        gain,
        enc_out,
        key_proj,
    )
    crossed = bands == 2
    sizes = SIZES if sum(SIZES) == share else [share]
    chains = len(sizes)
    offsets = [sum(sizes[:chain]) for chain in range(chains)]

    def kinds(group, carry=True):
        rows = group * key_dim
        pay = sds((rows + carry * carry_rows(group), val_dim), BF16)
        return sds((rows, val_dim), F32), sds((group, val_dim), F32), pay

    held = []
    for offset, group in zip(offsets, sizes):
        total, product, payload = call(
            functools.partial(state_body, share, crossed, offset), kinds(group)
        )(encoded, memory_in, turned, value_proj, rates)
        held.append((total, product, (), payload))
    conv = dec_conv.swapaxes(2, 3)
    late = [read_proj, conv.reshape(conv.shape[0], -1, conv.shape[3]), dec_up.T, spread]
    steps = (frames - 1).bit_length()
    for bit in range(steps):
        first, last = bit == 0, bit == steps - 1
        mask = 1 << bit
        turn = crossed and (mask & CROSSED_BITS).bit_count() % 2
        pairs = [
            (i * bands + c, (i ^ mask) * bands + (1 - c if turn else c))
            for i in range(frames)
            for c in range(bands)
            if i ^ mask < frames
        ]
        for chain, (total, product, carried, payload) in enumerate(held):
            arrived = lax.ppermute(payload, ("tm", "space"), pairs)
            if last:
                held[chain] = (arrived, total, product, *carried)
                ahead = payload
            else:
                state, small, pay = kinds(sizes[chain], bit < steps - 2)
                body = functools.partial(combine_body, bit, sizes[chain], first, False)
                total, product, reach, prefix, payload = call(
                    body, (state, small, small, state, pay)
                )(arrived, total, product, *carried)
                held[chain] = (total, product, (reach, prefix), payload)

    key_rows, *late = call(
        keys_body,
        (sds((window_rows, heads * key_dim), BF16), *[sds(x.shape, BF16) for x in late]),
        (pltpu.VMEM(key_proj.shape, BF16), pltpu.SemaphoreType.DMA((5,))),
        [pltpu.VMEM] * 2 + [pl.ANY] * (1 + len(late)),
    )(window, ahead, key_proj, *late)
    read_out, *late = late

    def read(firsts, arrays, begun):
        body = functools.partial(read_body, heads, firsts, len(begun))
        return [call(body, sds((window_rows, dim), F32))(key_rows, read_out, *begun, *arrays)]

    order, begun, pieces = key_rows, [], []
    for chain, operands in enumerate(held):
        body = functools.partial(combine_body, steps - 1, sizes[chain], steps == 1, True)
        memory = call(body, sds((sizes[chain] * key_dim, val_dim), BF16))(*operands, order)
        offset = offsets[chain]
        if bands == 2:
            pieces.append((functools.partial(own_first, share, offset, False), [memory]))
            other = lax.ppermute(memory, "space", swap)
            pieces.append((functools.partial(own_first, share, offset, True), [other]))
        else:
            every = lax.all_gather(memory, "space", axis=0)
            firsts = [band * share + offset for band in range(bands)]
            pieces.append((lambda firsts=firsts: firsts, [every[band] for band in range(bands)]))
        if chain < chains - 1:
            begun = read(*pieces.pop(0), begun)
            order = begun[0]
    for piece in pieces[:-1]:
        begun = read(*piece, begun)
    if not begun:
        begun = [jnp.zeros((window_rows, dim), F32)]
    firsts, arrays = pieces[-1]
    logits = call(
        functools.partial(decode_body, width, heads, firsts),
        jax.ShapeDtypeStruct((tile_rows * UP, width * UP), F32),
    )(key_rows, read_out, *begun, *arrays, window, *late)
    return logits[None]


def solution(mesh):
    return jax.shard_map(
        shards,
        mesh=mesh,
        in_specs=(
            P("tm", "space", None, None),
            P("space", None),
            P(),
            P(),
            P(),
            P(),
            P(),
            P(),
            P(),
            P("tm", None),
            P(),
            P(),
        ),
        out_specs=P("tm", "space", None),
        check_vma=False,
    )
```

```python
import functools

import jax
import jax.numpy as jnp
import numpy as np
from jax import lax
from jax.experimental import pallas as pl
from jax.experimental.pallas import tpu as pltpu
from jax.sharding import PartitionSpec as P

ENC_HEADS = 8
UP = 4
LANES = 128
ON_CHIP = 1 << 18
SIZES = [2, 2]
CROSSED_BITS = 1
EPSILON = 1e-06
F32 = jnp.float32
BF16 = jnp.bfloat16
VMEM = pl.BlockSpec(memory_space=pltpu.VMEM)


def dot(a, b):
    return jnp.dot(a, b, preferred_element_type=F32)


def dot_on(a, b, dim_a, dim_b, precision=None):
    return lax.dot_general(
        a, b, (((dim_a,), (dim_b,)), ((), ())), precision=precision, preferred_element_type=F32
    )


def call_in(chip, body, outs, scratch=(), spaces=None, micros=0):
    def result(x):
        shaped = jax.ShapeDtypeStruct(x.shape, x.dtype)
        return x if chip or isinstance(x, jax.ShapeDtypeStruct) else shaped

    outs = jax.tree.map(result, outs)

    def run(*operands):
        places = [pltpu.VMEM] * len(operands) if spaces is None else spaces
        kernel = pl.pallas_call(
            body,
            out_shape=outs,
            in_specs=[pl.BlockSpec(memory_space=place) for place in places],
            out_specs=jax.tree.map(lambda _: VMEM, outs),
            scratch_shapes=scratch,
            cost_estimate=pl.CostEstimate(
                flops=int(micros * 1e9), transcendentals=0, bytes_accessed=0
            ),
        )
        held = chip and pltpu.VMEM
        return kernel(
            *[
                pltpu.with_memory_space_constraint(x, place) if place is held else x
                for x, place in zip(operands, places)
            ]
        )

    return run


def own_band(crossed):
    band = lax.axis_index("space")
    if crossed:
        bits = lax.axis_index("tm") & CROSSED_BITS
        shift = 16
        while shift:
            bits = bits ^ (bits >> shift)
            shift //= 2
        band = (band + bits) & 1
    return band


def carry_rows(share):
    return -(-3 * share // 16) * 16


def split(x):
    high = x.astype(BF16).astype(F32)
    mid = (x - high).astype(BF16).astype(F32)
    low = (x - high - mid).astype(BF16).astype(F32)
    return [high, mid, low]


def write_payload(pay_ref, totals, product, share, key_dim):
    for h in range(share):
        rows = slice(h * key_dim, (h + 1) * key_dim)
        pay_ref[rows, :] = totals[h].astype(BF16)
    tail = pay_ref.shape[0] - share * key_dim
    if tail == 0:
        return
    parts = split(product)
    if tail > 3 * share:
        parts.append(jnp.zeros((tail - 3 * share, product.shape[1]), F32))
    pay_ref[share * key_dim :, :] = jnp.concatenate(parts, axis=0).astype(BF16)


def project_body(loaded, *refs):
    sources, targets = refs[:loaded], refs[loaded : 2 * loaded]
    query_ref, pair_ref, sems = refs[2 * loaded :]
    tile_ref, pool_ref, qkv_ref = targets[:3]
    dim = tile_ref.shape[1]
    loads = [
        pltpu.make_async_copy(source, target, sems.at[n])
        for n, (source, target) in enumerate(zip(sources, targets))
    ]
    for load in loads:
        load.start()
    loads[0].wait()
    loads[1].wait()
    pooled = dot(pool_ref[...], tile_ref[...]).astype(BF16)
    loads[2].wait()
    pair_ref[...] = dot(pooled, qkv_ref[:, dim:]).astype(BF16)
    query_ref[...] = dot(tile_ref[...], qkv_ref[:, :dim]).astype(BF16)
    for load in loads[3:]:
        load.wait()


def encode_body(width, parts, share, crossed, *refs):
    tiles, labels = refs[:parts], refs[parts : 2 * parts]
    rest = refs[2 * parts :]
    query_ref, pair_ref, pool_ref, qkv_ref, table_ref, gain_ref, out_ref, key_ref = rest[:8]
    value_ref, decay_ref = rest[8:10]
    window_ref, encoded_ref, memory_ref, turned_ref = rest[10:14]
    state_refs, padded = rest[14:-1], rest[-1]
    place = lax.axis_index("space")
    dim = query_ref.shape[1]
    size = dim // ENC_HEADS
    window_rows = window_ref.shape[0]
    tile_tok = window_rows - 2 * width
    queries, pairs = [query_ref[...]], [pair_ref[...]]
    for tile in tiles[1:]:
        queries.append(dot(tile[...], qkv_ref[:, :dim]).astype(BF16))
        pooled = dot(pool_ref[...], tile[...]).astype(BF16)
        pairs.append(dot(pooled, qkv_ref[:, dim:]).astype(BF16))
    x = jnp.concatenate([tile[...] for tile in tiles], axis=0)
    queries = jnp.concatenate(queries, axis=0)
    pair = jnp.concatenate(pairs, axis=0)
    tokens = x.shape[0]
    count = pair.shape[0]
    lane = lax.broadcasted_iota(jnp.int32, (count, dim), 1)
    masks = [(lane >= h * size) & (lane < (h + 1) * size) for h in range(ENC_HEADS)]
    zero = jnp.zeros((count, dim), BF16)
    keys = jnp.concatenate([jnp.where(m, pair[:, :dim], zero) for m in masks], axis=0)
    values = jnp.concatenate([jnp.where(m, pair[:, dim:], zero) for m in masks], axis=0)
    scores = (dot_on(keys, queries, 1, 1) * size ** (-0.5)).reshape(ENC_HEADS, count, tokens)
    weights = jnp.exp(scores - jnp.max(scores, axis=1, keepdims=True))
    totals = jnp.sum(weights, axis=1, keepdims=True)
    rounded = weights.astype(BF16).reshape(ENC_HEADS * count, tokens)
    summed = dot_on(values, rounded, 0, 0).reshape(ENC_HEADS, size, tokens)
    attended = (summed / totals).reshape(dim, tokens).astype(BF16)
    hidden = x.astype(F32) + dot_on(attended, out_ref[...], 0, 0)
    scale = lax.rsqrt(jnp.mean(hidden * hidden, axis=-1, keepdims=True) + EPSILON)
    encoded = (hidden * scale * gain_ref[...]).astype(BF16)
    encoded_ref[...] = encoded

    flag = (lax.axis_index("tm") == 0).astype(F32)
    kinds = table_ref.shape[0]
    label = jnp.concatenate(
        [ref[r : r + 1, :] for ref in labels for r in range(ref.shape[0])], axis=1
    )
    kind = lax.broadcasted_iota(jnp.int32, (kinds, tokens), 0)
    one_hot = (jnp.broadcast_to(label, (kinds, tokens)) == kind).astype(F32)
    one_hot = jnp.concatenate([one_hot] * 3, axis=0).astype(BF16)
    label_rows = dot_on(one_hot, jnp.concatenate(split(table_ref[...]), axis=0).astype(BF16), 0, 0)
    memory_ref[...] = (encoded.astype(F32) + flag * label_rows).astype(BF16)

    edge = jnp.zeros((width, dim), BF16)
    padded[:width, :] = edge
    padded[width + tokens :, :] = edge
    for p in range(parts):
        spot = place if p == 0 else 1 - place
        spot = pl.multiple_of(width + spot * tile_tok, width) if parts > 1 else width
        rows = tokens // parts
        padded[pl.ds(spot, rows), :] = encoded[p * rows : (p + 1) * rows]
    window_ref[...] = padded[pl.ds(pl.multiple_of(place * tile_tok, width), window_rows), :]
    cols = turned_ref.shape[0]
    start = pl.multiple_of(own_band(parts == 2) * cols, LANES)
    turned_ref[...] = key_ref[:, pl.ds(start, cols)].T
    state_body(
        share, crossed, 0, encoded_ref, memory_ref, turned_ref, value_ref, decay_ref, *state_refs
    )


def state_body(
    share, crossed, first_head, encoded_ref, memory_ref, turned_ref, value_ref, decay_ref, *out_refs
):
    state_ref, product_ref, pay_ref = out_refs
    heads = product_ref.shape[0]
    key_dim = turned_ref.shape[0] // share
    val_dim = state_ref.shape[1]
    tokens = encoded_ref.shape[0]
    cols = slice(first_head * key_dim, (first_head + heads) * key_dim)
    start = own_band(crossed) * share + first_head
    val_cols = pl.ds(pl.multiple_of(start * val_dim, val_dim), heads * val_dim)
    keys = dot_on(turned_ref[cols, :], encoded_ref[...], 1, 1).astype(BF16)
    values = dot(memory_ref[...], value_ref[:, val_cols]).astype(BF16)
    states = []
    for h in range(heads):
        state = dot(
            keys[h * key_dim : (h + 1) * key_dim], values[:, h * val_dim : (h + 1) * val_dim]
        ) * tokens ** (-0.5)
        state_ref[h * key_dim : (h + 1) * key_dim, :] = state
        states.append(state)
    rates = jnp.broadcast_to(decay_ref[...], (heads, decay_ref.shape[1]))
    head = lax.broadcasted_iota(jnp.int32, rates.shape, 0) + start
    picked = lax.broadcasted_iota(jnp.int32, rates.shape, 1) == head
    rate = jnp.sum(jnp.where(picked, rates, jnp.zeros_like(rates)), axis=1, keepdims=True)
    product = jnp.broadcast_to(rate, (heads, val_dim))
    product_ref[...] = product
    write_payload(pay_ref, states, product, heads, key_dim)


def combine_body(bit, share, first, last, recv_ref, total_ref, product_ref, *refs):
    if not first:
        reach_ref, prefix_ref = refs[:2]
    outs = refs[-1:] if last else refs[-5:]
    rows = total_ref.shape[0]
    key_dim = rows // share
    upper = (lax.axis_index("tm") >> bit) & 1
    is_upper = jnp.full(product_ref.shape, upper, jnp.int32) == 1
    product = product_ref[...]
    reach = product if first else reach_ref[...]
    if not last:
        tail = recv_ref[rows:, :].astype(F32)
        got = tail[:share] + tail[share : 2 * share] + tail[2 * share : 3 * share]
        ones = jnp.ones_like(product)
        on_got = jnp.where(is_upper, product, ones)
        on_own = jnp.where(is_upper, ones, got)
    on_prefix = jnp.where(is_upper, reach, jnp.zeros_like(product))
    totals = []
    for h in range(share):
        part = slice(h * key_dim, (h + 1) * key_dim)
        arrived = recv_ref[part, :].astype(F32)
        prefix = on_prefix[h : h + 1] * arrived
        if not first:
            prefix = prefix + prefix_ref[part, :]
        if last:
            outs[0][part, :] = prefix.astype(BF16)
        else:
            outs[3][part, :] = prefix
            total = on_got[h : h + 1] * arrived + on_own[h : h + 1] * total_ref[part, :]
            totals.append(total)
            outs[0][part, :] = total
    if not last:
        joined = product * got
        outs[1][...] = joined
        outs[2][...] = jnp.where(is_upper, reach * got, reach)
        write_payload(outs[4], totals, joined, share, key_dim)


def keys_body(window_ref, after, key_hbm, *refs):
    count = (len(refs) - 3) // 2
    sources, out_ref, targets, (key_ref, sems) = (
        refs[:count],
        refs[count],
        refs[count + 1 : -2],
        refs[-2:],
    )
    loads = [
        pltpu.make_async_copy(source, target, sems.at[n])
        for n, (source, target) in enumerate(zip((key_hbm, *sources), (key_ref, *targets)))
    ]
    for load in loads:
        load.start()
    loads[0].wait()
    out_ref[...] = dot(window_ref[...], key_ref[...]).astype(BF16)
    for load in loads[1:]:
        load.wait()


def read_rows(heads, firsts, key_ref, read_ref, memories):
    key_dim = key_ref.shape[1] // heads
    total = None
    for first, memory_ref in zip(firsts, memories):
        count = memory_ref.shape[0] // key_dim
        start = first * key_dim
        start = start if isinstance(start, int) else pl.multiple_of(start, key_dim)
        keys = key_ref[:, pl.ds(start, count * key_dim)]
        reads = [
            dot(
                keys[:, h * key_dim : (h + 1) * key_dim],
                memory_ref[h * key_dim : (h + 1) * key_dim, :],
            )
            * key_dim ** (-0.5)
            for h in range(count)
        ]
        val_dim = memory_ref.shape[1]
        start = first * val_dim
        start = start if isinstance(start, int) else pl.multiple_of(start, val_dim)
        readout = jnp.concatenate(reads, axis=1).astype(BF16)
        piece = dot(readout, read_ref[pl.ds(start, count * val_dim), :])
        total = piece if total is None else total + piece
    return total


def own_first(share, offset, flip):
    place = own_band(True)
    return [(1 - place if flip else place) * share + offset]


def read_body(heads, firsts, begun, *refs):
    out_ref = refs[-1]
    key_ref, read_ref = refs[:2]
    memories = refs[2 + begun : -1]
    total = read_rows(heads, firsts(), key_ref, read_ref, memories)
    out_ref[...] = refs[2][...] + total if begun else total


def decode_body(width, heads, firsts, key_ref, read_ref, begun_ref, *refs):
    memories = refs[:-5]
    window_ref, conv_ref, up_ref, spread_ref, out_ref = refs[-5:]
    rows = window_ref.shape[0]
    tile_tok = rows - 2 * width
    total = read_rows(heads, firsts(), key_ref, read_ref, memories) + begun_ref[...]
    joined = (window_ref[...].astype(F32) + total).astype(BF16)
    summed = dot_on(joined[:tile_tok], conv_ref[0], 1, 1)
    for a in range(1, 3):
        summed = summed + dot_on(joined[a * width : a * width + tile_tok], conv_ref[a], 1, 1)
    chans = summed.shape[1] // 3
    columns = [summed[:, b * chans : (b + 1) * chans] for b in range(3)]
    col = lax.broadcasted_iota(jnp.int32, columns[0].shape, 0) % width
    zero = jnp.zeros_like(columns[0])
    left = jnp.where(col == 0, zero, pltpu.roll(columns[0], 1, 0))
    right = jnp.where(col == width - 1, zero, pltpu.roll(columns[2], tile_tok - 1, 0))
    mapped = jax.nn.gelu(left + columns[1] + right).astype(BF16)
    wide = tile_tok * UP
    lane = lax.broadcasted_iota(jnp.int32, (UP, UP, wide), 2)
    sub = lax.broadcasted_iota(jnp.int32, (UP, UP, wide), 1)
    small = jnp.concatenate(split(dot_on(up_ref[...], mapped, 1, 1)), axis=0).astype(BF16)
    parts = dot(small, spread_ref[...]).reshape(3, UP, UP, wide)
    pixels = parts[0] + parts[1] + parts[2]
    picked = jnp.sum(jnp.where((lane % UP) == sub, pixels, jnp.zeros_like(pixels)), axis=1)
    line = width * UP
    for i in range(tile_tok // width):
        out_ref[i * UP : (i + 1) * UP, :] = picked[:, i * line : (i + 1) * line]


def shards(
    frames_feat,
    prompt_labels,
    label_table,
    enc_qkv,
    enc_out,
    norm_gain,
    key_proj,
    value_proj,
    read_proj,
    decay,
    dec_conv,
    dec_up,
):
    _, tile_rows, width, dim = frames_feat.shape
    tile_tok = tile_rows * width
    bands, frames = lax.axis_size("space"), lax.axis_size("tm")
    tokens = tile_tok * bands
    heads = decay.shape[1]
    share = heads // bands
    key_dim, val_dim = key_proj.shape[1] // heads, value_proj.shape[1] // heads
    window_rows = tile_tok + 2 * width
    sds = pltpu.VMEM
    call = functools.partial(call_in, 2 * tokens * dim <= ON_CHIP)

    flat = frames_feat.reshape(tile_tok, dim)
    swap = [(0, 1), (1, 0)]
    if bands == 2:
        tiles = [flat, lax.ppermute(flat, "space", swap)]
        marks = [prompt_labels, lax.ppermute(prompt_labels, "space", swap)]
    else:
        tiles = [lax.all_gather(flat, "space", axis=0, tiled=True)]
        marks = [lax.all_gather(prompt_labels, "space", axis=0, tiled=True)]
    parts = len(tiles)
    tile = tiles[0].shape

    token = np.arange(tile[0])
    cell = (token // width // 2) * (width // 2) + token % width // 2
    pool = jnp.asarray((cell[None, :] == np.arange(tile[0] // 4)[:, None]) * 0.25, BF16)
    wide = np.arange(tile_tok * UP)
    row = wide // (width * UP) * width + wide % (width * UP) // UP
    spread = jnp.asarray(row[None, :] == np.arange(tile_tok)[:, None], BF16)

    gain = norm_gain.reshape(1, dim)
    loaded = [tiles[0], pool, enc_qkv, marks[0], label_table, gain, decay]
    tiles[0], pool, qkv, marks[0], table, gain, rates, queries, pairs = call(
        functools.partial(project_body, len(loaded)),
        (
            *[sds(x.shape, x.dtype) for x in loaded],
            sds(tile, BF16),
            sds((tile[0] // 4, 2 * dim), BF16),
        ),
        (pltpu.SemaphoreType.DMA((len(loaded),)),),
        [pl.ANY] * len(loaded),
        micros=1,
    )(*loaded)
    crossed = bands == 2
    sizes = SIZES if sum(SIZES) == share else [share]
    chains = len(sizes)
    offsets = [sum(sizes[:chain]) for chain in range(chains)]

    def kinds(group, carry=True):
        rows = group * key_dim
        pay = sds((rows + carry * carry_rows(group), val_dim), BF16)
        return sds((rows, val_dim), F32), sds((group, val_dim), F32), pay

    window, encoded, memory_in, turned, *opening = call(
        functools.partial(encode_body, width, parts, share, crossed),
        (
            sds((window_rows, dim), BF16),
            sds((tokens, dim), BF16),
            sds((tokens, dim), BF16),
            sds((share * key_dim, dim), BF16),
            *kinds(sizes[0]),
        ),
        (pltpu.VMEM((tokens + 2 * width, dim), BF16),),
        micros=2,
    )(
        *tiles,
        *marks,
        queries,
        pairs,
        pool,
        qkv,
        table,
        gain,
        enc_out,
        key_proj,
        value_proj,
        rates,
    )
    held = [(opening[0], opening[1], (), opening[2])]
    for offset, group in zip(offsets[1:], sizes[1:]):
        total, product, payload = call(
            functools.partial(state_body, share, crossed, offset), kinds(group)
        )(encoded, memory_in, turned, value_proj, rates)
        held.append((total, product, (), payload))
    conv = dec_conv.swapaxes(2, 3)
    late = [read_proj, conv.reshape(conv.shape[0], -1, conv.shape[3]), dec_up.T, spread]
    steps = (frames - 1).bit_length()
    for bit in range(steps):
        first, last = bit == 0, bit == steps - 1
        mask = 1 << bit
        turn = crossed and (mask & CROSSED_BITS).bit_count() % 2
        pairs = [
            (i * bands + c, (i ^ mask) * bands + (1 - c if turn else c))
            for i in range(frames)
            for c in range(bands)
            if i ^ mask < frames
        ]
        for chain, (total, product, carried, payload) in enumerate(held):
            arrived = lax.ppermute(payload, ("tm", "space"), pairs)
            if last:
                held[chain] = (arrived, total, product, *carried)
                ahead = payload
            else:
                state, small, pay = kinds(sizes[chain], bit < steps - 2)
                body = functools.partial(combine_body, bit, sizes[chain], first, False)
                total, product, reach, prefix, payload = call(
                    body, (state, small, small, state, pay)
                )(arrived, total, product, *carried)
                held[chain] = (total, product, (reach, prefix), payload)

    key_rows, *late = call(
        keys_body,
        (sds((window_rows, heads * key_dim), BF16), *[sds(x.shape, BF16) for x in late]),
        (pltpu.VMEM(key_proj.shape, BF16), pltpu.SemaphoreType.DMA((5,))),
        [pltpu.VMEM] * 2 + [pl.ANY] * (1 + len(late)),
        micros=1,
    )(window, ahead, key_proj, *late)
    read_out, *late = late

    def read(firsts, arrays, begun):
        body = functools.partial(read_body, heads, firsts, len(begun))
        return [call(body, sds((window_rows, dim), F32))(key_rows, read_out, *begun, *arrays)]

    order, begun, pieces = key_rows, [], []
    for chain, operands in enumerate(held):
        body = functools.partial(combine_body, steps - 1, sizes[chain], steps == 1, True)
        memory = call(body, sds((sizes[chain] * key_dim, val_dim), BF16))(*operands, order)
        offset = offsets[chain]
        if bands == 2:
            pieces.append((functools.partial(own_first, share, offset, False), [memory]))
            other = lax.ppermute(memory, "space", swap)
            pieces.append((functools.partial(own_first, share, offset, True), [other]))
        else:
            every = lax.all_gather(memory, "space", axis=0)
            firsts = [band * share + offset for band in range(bands)]
            pieces.append((lambda firsts=firsts: firsts, [every[band] for band in range(bands)]))
        if chain < chains - 1:
            begun = read(*pieces.pop(0), begun)
            order = begun[0]
    for piece in pieces[:-1]:
        begun = read(*piece, begun)
    if not begun:
        begun = [jnp.zeros((window_rows, dim), F32)]
    firsts, arrays = pieces[-1]
    logits = call(
        functools.partial(decode_body, width, heads, firsts),
        jax.ShapeDtypeStruct((tile_rows * UP, width * UP), F32),
    )(key_rows, read_out, *begun, *arrays, window, *late)
    return logits[None]


def solution(mesh):
    return jax.shard_map(
        shards,
        mesh=mesh,
        in_specs=(
            P("tm", "space", None, None),
            P("space", None),
            P(),
            P(),
            P(),
            P(),
            P(),
            P(),
            P(),
            P("tm", None),
            P(),
            P(),
        ),
        out_specs=P("tm", "space", None),
        check_vma=False,
    )
```
